256 devices in a mesh: tm: 64 (over z_hi, y, x), head: 4 (over z_lo, core).
Axes of the slice: x: 4, y: 4, z: 8 (z_hi: 4, z_lo: 2; z = z_hi * 2 + z_lo), core: 2. Of those that a mesh axis runs over, the one named last changes fastest.
Arguments:
- query: bfloat16 [16384, 4096], P('tm', 'head'), may hold values from -200 to 200
- key_in: bfloat16 [16384, 4096], P('tm', 'head'), may hold values from -7 to 7
- value: bfloat16 [16384, 4096], P('tm', 'head'), may hold values from -6 to 6
- grad_out: bfloat16 [16384, 4096], P('tm', 'head'), may hold values from -6 to 6
- weights: bfloat16 [3, 4096, 4096], P(None, 'tm', 'head'), may hold values from -0.09375 to 0.09375
Outputs:
- grad_input_t: bfloat16 [4096, 16384], P('head', 'tm')
The draws below stay inside these ranges and needn't reach their ends.
All inputs are finite; a program needn't handle non-finite values.
Results may differ from the reference program's by a relative error of at most 0.0091.
Values may be sent and summed in bfloat16 or wider, within the bound.
A program may use at most 256 MiB of HBM per device.

```python
import jax
import jax.numpy as jnp
from jax import lax

D = 4096
HEADS = 32
HD = 128
PATCHES = 256
FRAMES = 64
TOKENS = 16384


def paired_draw(key):
    base_q = jnp.clip(jax.random.normal(jax.random.fold_in(key, 11), (TOKENS, D), jnp.float32), -6.0, 6.0)
    base_k = jnp.clip(jax.random.normal(jax.random.fold_in(key, 12), (TOKENS, D), jnp.float32), -6.0, 6.0)
    keys = base_k
    queries = base_q
    return (queries, keys)


def draw_query(key, part):
    return paired_draw(key)[0].astype(jnp.bfloat16)


def draw_key_in(key, part):
    return paired_draw(key)[1].astype(jnp.bfloat16)


def levels(stream_key, extent, pieces, least, high):
    def one(axis_at, blocks):
        heights = jax.random.uniform(jax.random.fold_in(jax.random.fold_in(stream_key, 6), axis_at), (blocks,), jnp.float32, least / len(pieces), high / len(pieces))
        return jnp.repeat(jnp.exp(heights), extent[axis_at] // blocks).reshape((-1,) + (1,) * (len(extent) - axis_at - 1))

    level = one(*pieces[0])
    for cut in pieces[1:]:
        level = level * one(*cut)
    return level


def noise(key, extent, spread, limit, shards=(), kind=jnp.bfloat16):
    loudness = levels(key, extent, shards, -0.22, 0.18) if shards else 1.0
    values = jax.random.normal(key, extent, jnp.float32) * spread * loudness
    return jnp.minimum(jnp.maximum(values, -limit), limit).astype(kind)


def setup_inputs(seed: int = 0) -> dict:
    arg_keys = jax.random.split(jax.random.key(seed), 6)
    query = draw_query(jax.random.fold_in(arg_keys[5], 71), 0)
    key_in = draw_key_in(jax.random.fold_in(arg_keys[5], 71), 0)
    value = noise(arg_keys[2], (TOKENS, D), 1.0, 6.0, ((0, 64), (1, 4)))
    grad_out = noise(arg_keys[3], (TOKENS, D), 1.0, 6.0, ((0, 64), (1, 4)))
    weights = noise(arg_keys[4], (3, D, D), D ** -0.5, 0.09375, ((1, 64), (2, 4)))
    return {"query": query, "key_in": key_in, "value": value, "grad_out": grad_out, "weights": weights}


def round_keep(array):
    return lax.optimization_barrier(array.astype(jnp.bfloat16)).astype(jnp.float32)


def reference(query, key_in, value, grad_out, weights):
    scale = 1.0 / (HD ** 0.5)

    def heads(array):
        return array.astype(jnp.float32).reshape(FRAMES, PATCHES, HEADS, HD)

    q_heads = heads(query)
    k_heads = heads(key_in)
    v_heads = heads(value)
    g_heads = heads(grad_out)
    scores = jnp.einsum("fphd,gphd->phfg", q_heads, k_heads) * scale
    probs = jax.nn.softmax(scores, axis=-1)
    probs_b = round_keep(probs)
    attended = jnp.einsum("phfg,gphd->fphd", probs_b, v_heads)
    delta = jnp.transpose(jnp.sum(g_heads * attended, axis=-1), (1, 2, 0))
    grad_probs = jnp.einsum("fphd,gphd->phfg", g_heads, v_heads)
    grad_scores = round_keep(probs * (grad_probs - delta[..., None]))
    grad_value = jnp.einsum("phfg,fphd->gphd", probs_b, g_heads).astype(jnp.bfloat16)
    grad_query = (jnp.einsum("phfg,gphd->fphd", grad_scores, k_heads) * scale).astype(jnp.bfloat16)
    grad_key = (jnp.einsum("phfg,fphd->gphd", grad_scores, q_heads) * scale).astype(jnp.bfloat16)
    grads = [grad_query, grad_key, grad_value]
    total = jnp.zeros((D, TOKENS), jnp.float32)
    for which in range(3):
        flat = grads[which].reshape(TOKENS, D)
        total = total + jnp.dot(weights[which], flat.T, preferred_element_type=jnp.float32)
    return total.astype(jnp.bfloat16)
```

```python
import jax
import jax.numpy as jnp
import numpy as np
from jax import lax
from jax.experimental import pallas as pl
from jax.experimental.pallas import tpu as pltpu
from jax.sharding import Mesh, PartitionSpec as P

HD = 128
AXES = ("z", "yh", "yl", "xh", "xl", "zl", "c")
TM = AXES[:5]
HEAD = AXES[5:]
BF16 = jnp.bfloat16
F32 = jnp.float32
BY_MESH = pl.DeviceIdType.MESH
ANY = pl.BlockSpec(memory_space=pl.ANY)


def position():
    at = lax.axis_index
    return at("z"), 2 * at("yh") + at("yl"), 2 * at("xh") + at("xl")


def device(z, y, x):
    return {"z": z, "yh": y // 2, "yl": y % 2, "xh": x // 2, "xl": x % 2}


def partner(at, shift):
    return (at + 1 + 2 * ((at + shift) % 2)) % 4


def swap_kernel(src, dst, send_sem, recv_sem, own_sem):
    z, y, x = position()
    me = z * 16 + y * 4 + x
    own = pltpu.make_async_copy(src.at[me], dst.at[me], own_sem)
    own.start()
    barrier = pltpu.get_barrier_semaphore()

    def peer(step):
        return (z + step // 16) % 4, (y + (step // 4) % 4) % 4, (x + step % 4) % 4

    def greet(step, carry):
        pl.semaphore_signal(barrier, inc=1, device_id=device(*peer(step)), device_id_type=BY_MESH)
        return carry

    lax.fori_loop(1, 64, greet, 0)
    pl.semaphore_wait(barrier, 63)

    def send(step, carry):
        pz, py, px = peer(step)
        pltpu.make_async_remote_copy(
            src_ref=src.at[pz * 16 + py * 4 + px],
            dst_ref=dst.at[me],
            send_sem=send_sem,
            recv_sem=recv_sem,
            device_id=device(pz, py, px),
            device_id_type=BY_MESH,
        ).start()
        return carry

    lax.fori_loop(1, 64, send, 0)
    most = pl.ds(0, 63)
    pltpu.make_async_copy(src.at[most], src.at[most], send_sem).wait()
    pltpu.make_async_copy(dst.at[most], dst.at[most], recv_sem).wait()
    own.wait()


def swap(array, collective_id):
    return pl.pallas_call(
        swap_kernel,
        out_shape=jax.ShapeDtypeStruct(array.shape, array.dtype),
        in_specs=[ANY],
        out_specs=ANY,
        scratch_shapes=[pltpu.SemaphoreType.DMA] * 3,
        compiler_params=pltpu.CompilerParams(collective_id=collective_id, has_side_effects=True),
        name=f"swap_{collective_id}",
    )(array)


def share_kernel(src, dst, send_sem, recv_sem, own_sem):
    z, y, x = position()
    slot = (y % 2) * 2 + x % 2
    own = pltpu.make_async_copy(src, dst.at[:, slot], own_sem)
    own.start()
    barrier = pltpu.get_barrier_semaphore()
    for dy, dx in ((0, 1), (0, 3), (1, 0), (3, 0), (1, 1), (1, 3), (3, 1), (3, 3)):
        pl.semaphore_signal(
            barrier, inc=1, device_id=device(z, (y + dy) % 4, (x + dx) % 4), device_id_type=BY_MESH
        )
    pl.semaphore_wait(barrier, 8)
    copies = []
    for role in (2, 0, 1):
        for c in range(4):
            py, px = partner(y, c // 2), partner(x, c % 2)
            target = (device(z, y, px), device(z, py, x), device(z, py, px))[role]
            copy = pltpu.make_async_remote_copy(
                src_ref=src.at[:, c],
                dst_ref=dst.at[:, slot, c],
                send_sem=send_sem.at[role, c],
                recv_sem=recv_sem.at[role, c],
                device_id=target,
                device_id_type=BY_MESH,
            )
            copy.start()
            copies.append(copy)
    for copy in copies:
        copy.wait()
    own.wait()


def share(grads):
    m, c, f, k = grads.shape
    return pl.pallas_call(
        share_kernel,
        out_shape=jax.ShapeDtypeStruct((m, 4, c, f, k), grads.dtype),
        in_specs=[ANY],
        out_specs=ANY,
        scratch_shapes=[
            pltpu.SemaphoreType.DMA((3, 4)),
            pltpu.SemaphoreType.DMA((3, 4)),
            pltpu.SemaphoreType.DMA,
        ],
        compiler_params=pltpu.CompilerParams(collective_id=3, has_side_effects=True),
        name="share",
    )(grads)


def patch_order():
    place = np.zeros((4, 256, 256), np.float32)
    for yl in range(2):
        for xl in range(2):
            row = 0
            for z in range(4):
                for yh in range(2):
                    for xh in range(2):
                        y, x = 2 * yh + yl, 2 * xh + xl
                        for slot in range(4):
                            for c in range(4):
                                ys = y if slot // 2 == yl else partner(y, c // 2)
                                xs = x if slot % 2 == xl else partner(x, c % 2)
                                place[yl * 2 + xl, row, 4 * (z * 16 + ys * 4 + xs) + c] = 1
                                row += 1
    return place


def temporal(q_heads, k_heads, v_heads, g_heads):
    scale = 1.0 / q_heads.shape[-1] ** 0.5
    scores = (
        jnp.einsum("fphd,gphd->phfg", q_heads, k_heads, preferred_element_type=F32) * scale
    )
    probs = jax.nn.softmax(scores, axis=-1)
    probs_b = probs.astype(BF16)
    attended = jnp.einsum("phfg,gphd->fphd", probs_b, v_heads, preferred_element_type=F32)
    delta = jnp.transpose(jnp.sum(g_heads.astype(F32) * attended, axis=-1), (1, 2, 0))
    grad_probs = jnp.einsum("fphd,gphd->phfg", g_heads, v_heads, preferred_element_type=F32)
    grad_scores = (probs * (grad_probs - delta[..., None])).astype(BF16)
    grad_value = jnp.einsum("phfg,fphd->pghd", probs_b, g_heads, preferred_element_type=F32)
    grad_query = (
        jnp.einsum("phfg,gphd->pfhd", grad_scores, k_heads, preferred_element_type=F32) * scale
    )
    grad_key = (
        jnp.einsum("phfg,fphd->pghd", grad_scores, q_heads, preferred_element_type=F32) * scale
    )
    return grad_query.astype(BF16), grad_key.astype(BF16), grad_value.astype(BF16)


def per_device(query, key_in, value, grad_out, weights):
    rows = lax.all_gather(weights, ("z", "yh", "xh"), axis=1, tiled=True)
    packed = jnp.stack([a.reshape(64, 4, 1024) for a in (query, key_in, value, grad_out)], axis=1)
    moved = swap(packed.reshape(64, 16, 1024), 1).reshape(64, 4, 4, 8, HD)
    grads = temporal(moved[:, 0], moved[:, 1], moved[:, 2], moved[:, 3])
    stacked = jnp.stack([a.reshape(4, 64, 1024) for a in grads])
    shared = share(stacked).reshape(3, 1024, 1024)
    partial_sum = jnp.einsum(
        "mtk,mzik->zti", shared, rows.reshape(3, 4, 256, 1024), preferred_element_type=F32
    ).astype(BF16)
    mine = lax.psum_scatter(partial_sum, HEAD, scatter_dimension=0, tiled=True)
    by_frame = jnp.transpose(mine.reshape(16, 64, 256), (1, 0, 2))
    back = swap(by_frame, 2).reshape(4, 2, 2, 2, 2, 16, 2, 2, 64)
    place = jnp.asarray(patch_order(), BF16).reshape(2, 2, 4, 2, 2, 16, 256)
    out = jnp.einsum("zybxatvuk,bazyxtp->vbuakp", back, place, preferred_element_type=F32)
    return out.reshape(1024, 256).astype(BF16)


def solution(mesh):
    fine = Mesh(mesh.devices.reshape(4, 2, 2, 2, 2, 2, 2), AXES)
    placed = (P(TM, HEAD),) * 4 + (P(None, TM, HEAD),)
    return jax.shard_map(
        per_device, mesh=fine, in_specs=placed, out_specs=P(HEAD, TM), check_vma=False
    )
```

```python
import functools

import jax
import jax.numpy as jnp
import numpy as np
from jax import lax
from jax.experimental import pallas as pl
from jax.experimental.pallas import tpu as pltpu
from jax.sharding import Mesh, PartitionSpec as P

HD = 128
AXES = ("z", "y", "x", "zl", "c")
TM = AXES[:3]
HEAD = AXES[3:]
BF16 = jnp.bfloat16
F32 = jnp.float32
BY_MESH = pl.DeviceIdType.MESH
ANY = pl.BlockSpec(memory_space=pl.ANY)


def position():
    return lax.axis_index("z"), lax.axis_index("y"), lax.axis_index("x")


def swap_kernel(y_major, src, dst, send_sem, recv_sem, own_sem):
    z, y, x = position()
    me = z * 16 + y * 4 + x
    slot = y * 16 + z * 4 + x if y_major else me
    own = pltpu.make_async_copy(src.at[me], dst.at[slot], own_sem)
    own.start()
    barrier = pltpu.get_barrier_semaphore()

    def peer(step):
        return (z + step // 16) % 4, (y + (step // 4) % 4) % 4, (x + step % 4) % 4

    def greet(step, carry):
        pl.semaphore_signal(barrier, inc=1, device_id=dict(zip(TM, peer(step))), device_id_type=BY_MESH)
        return carry

    lax.fori_loop(1, 64, greet, 0)
    pl.semaphore_wait(barrier, 63)

    def send(step, carry):
        pz, py, px = peer(step)
        pltpu.make_async_remote_copy(
            src_ref=src.at[pz * 16 + py * 4 + px],
            dst_ref=dst.at[slot],
            send_sem=send_sem,
            recv_sem=recv_sem,
            device_id={"z": pz, "y": py, "x": px},
            device_id_type=BY_MESH,
        ).start()
        return carry

    lax.fori_loop(1, 64, send, 0)
    most = pl.ds(0, 63)
    pltpu.make_async_copy(src.at[most], src.at[most], send_sem).wait()
    pltpu.make_async_copy(dst.at[most], dst.at[most], recv_sem).wait()
    own.wait()


def swap(array, collective_id, y_major):
    return pl.pallas_call(
        functools.partial(swap_kernel, y_major),
        out_shape=jax.ShapeDtypeStruct(array.shape, array.dtype),
        in_specs=[ANY],
        out_specs=ANY,
        scratch_shapes=[pltpu.SemaphoreType.DMA] * 3,
        compiler_params=pltpu.CompilerParams(collective_id=collective_id, has_side_effects=True),
        name=f"swap_{collective_id}",
    )(array)


def share_kernel(src, dst, send_sem, recv_sem, own_sem):
    y = lax.axis_index("y")
    up, down = (y + 1) % 4, (y + 3) % 4
    own = pltpu.make_async_copy(src, dst.at[:, y], own_sem)
    own.start()
    barrier = pltpu.get_barrier_semaphore()
    for target in (up, down):
        pl.semaphore_signal(barrier, inc=1, device_id={"y": target}, device_id_type=BY_MESH)
    pl.semaphore_wait(barrier, 2)

    def send(block, slot, c, target, lane):
        copy = pltpu.make_async_remote_copy(
            src_ref=block,
            dst_ref=dst.at[:, slot, c],
            send_sem=send_sem.at[lane, c],
            recv_sem=recv_sem.at[lane, c],
            device_id={"y": target},
            device_id_type=BY_MESH,
        )
        copy.start()
        return copy

    ups, downs, far = {}, {}, []
    for step in range(4):
        c, d = step, (step + 2) % 4
        ups[c] = send(src.at[:, c], y, c, up, 0)
        downs[d] = send(src.at[:, d], y, d, down, 1)
    for step in range(2):
        c, d = step, step + 2
        ups[c].wait_recv()
        far.append(send(dst.at[:, down, c], down, c, up, 2))
        downs[d].wait_recv()
        far.append(send(dst.at[:, up, d], up, d, down, 2))
    for step in range(2):
        ups[step + 2].wait_recv()
        downs[step].wait_recv()
    for copy in far:
        copy.wait_recv()
    for copy in (*ups.values(), *downs.values(), *far):
        copy.wait_send()
    own.wait()


def share(grads):
    m, c, f, k = grads.shape
    return pl.pallas_call(
        share_kernel,
        out_shape=jax.ShapeDtypeStruct((m, 4, c, f, k), grads.dtype),
        in_specs=[ANY],
        out_specs=ANY,
        scratch_shapes=[
            pltpu.SemaphoreType.DMA((3, 4)),
            pltpu.SemaphoreType.DMA((3, 4)),
            pltpu.SemaphoreType.DMA,
        ],
        compiler_params=pltpu.CompilerParams(collective_id=3, has_side_effects=True),
        name="share",
    )(grads)


def patch_order():
    z, x, slot, c = np.indices((4, 4, 4, 4)).reshape(4, 256)
    return np.eye(256, dtype=np.float32)[4 * (z * 16 + slot * 4 + x) + c]


def temporal(q_heads, k_heads, v_heads, g_heads):
    scale = 1.0 / q_heads.shape[-1] ** 0.5
    scores = (
        jnp.einsum("fphd,gphd->phfg", q_heads, k_heads, preferred_element_type=F32) * scale
    )
    probs = jax.nn.softmax(scores, axis=-1)
    probs_b = probs.astype(BF16)
    attended = jnp.einsum("phfg,gphd->fphd", probs_b, v_heads, preferred_element_type=F32)
    delta = jnp.transpose(jnp.sum(g_heads.astype(F32) * attended, axis=-1), (1, 2, 0))
    grad_probs = jnp.einsum("fphd,gphd->phfg", g_heads, v_heads, preferred_element_type=F32)
    grad_scores = (probs * (grad_probs - delta[..., None])).astype(BF16)
    grad_value = jnp.einsum("phfg,fphd->pghd", probs_b, g_heads, preferred_element_type=F32)
    grad_query = (
        jnp.einsum("phfg,gphd->pfhd", grad_scores, k_heads, preferred_element_type=F32) * scale
    )
    grad_key = (
        jnp.einsum("phfg,fphd->pghd", grad_scores, q_heads, preferred_element_type=F32) * scale
    )
    return grad_query.astype(BF16), grad_key.astype(BF16), grad_value.astype(BF16)


def per_device(query, key_in, value, grad_out, weights):
    rows = lax.all_gather(weights, ("z", "x"), axis=1, tiled=True)
    packed = jnp.stack([a.reshape(64, 4, 1024) for a in (query, key_in, value, grad_out)], axis=1)
    moved = swap(packed.reshape(64, 16, 1024), 1, False).reshape(64, 4, 4, 8, HD)
    grads = temporal(moved[:, 0], moved[:, 1], moved[:, 2], moved[:, 3])
    stacked = jnp.stack([a.reshape(4, 64, 1024) for a in grads])
    shared = share(stacked).reshape(3, 1024, 1024)
    partial_sum = jnp.einsum(
        "mtk,mzik->zti", shared, rows.reshape(3, 4, 256, 1024), preferred_element_type=F32
    ).astype(BF16)
    mine = lax.psum_scatter(partial_sum, HEAD, scatter_dimension=0, tiled=True)
    by_frame = jnp.transpose(mine.reshape(16, 64, 256), (1, 0, 2))
    back = swap(by_frame, 2, True).reshape(4, 256, 256)
    place = jnp.asarray(patch_order(), BF16)
    out = jnp.einsum("ytk,tp->ykp", back, place, preferred_element_type=F32)
    return out.reshape(1024, 256).astype(BF16)


def solution(mesh):
    fine = Mesh(mesh.devices.reshape(4, 4, 4, 2, 2), AXES)
    placed = (P(TM, HEAD),) * 4 + (P(None, TM, HEAD),)
    return jax.shard_map(
        per_device, mesh=fine, in_specs=placed, out_specs=P(HEAD, TM), check_vma=False
    )
```

```python
import jax
import jax.numpy as jnp
import numpy as np
from jax import lax
from jax.experimental import pallas as pl
from jax.experimental.pallas import tpu as pltpu
from jax.sharding import Mesh, PartitionSpec as P

HD = 128
AXES = ("z", "y", "x", "zl", "c")
TM = AXES[:3]
HEAD = AXES[3:]
BF16 = jnp.bfloat16
F32 = jnp.float32
BY_MESH = pl.DeviceIdType.MESH
ANY = pl.BlockSpec(memory_space=pl.ANY)


def position():
    return lax.axis_index("z"), lax.axis_index("y"), lax.axis_index("x")


def swap_kernel(src, dst, send_sem, recv_sem, own_sem):
    z, y, x = position()
    me = z * 16 + y * 4 + x
    own = pltpu.make_async_copy(src.at[me], dst.at[me], own_sem)
    own.start()
    barrier = pltpu.get_barrier_semaphore()

    def peer(step):
        return (z + step // 16) % 4, (y + (step // 4) % 4) % 4, (x + step % 4) % 4

    def greet(step, carry):
        pl.semaphore_signal(barrier, inc=1, device_id=dict(zip(TM, peer(step))), device_id_type=BY_MESH)
        return carry

    lax.fori_loop(1, 64, greet, 0)
    pl.semaphore_wait(barrier, 63)

    def send(step, carry):
        pz, py, px = peer(step)
        pltpu.make_async_remote_copy(
            src_ref=src.at[pz * 16 + py * 4 + px],
            dst_ref=dst.at[me],
            send_sem=send_sem,
            recv_sem=recv_sem,
            device_id={"z": pz, "y": py, "x": px},
            device_id_type=BY_MESH,
        ).start()
        return carry

    lax.fori_loop(1, 64, send, 0)
    most = pl.ds(0, 63)
    pltpu.make_async_copy(src.at[most], src.at[most], send_sem).wait()
    pltpu.make_async_copy(dst.at[most], dst.at[most], recv_sem).wait()
    own.wait()


def swap(array, collective_id):
    return pl.pallas_call(
        swap_kernel,
        out_shape=jax.ShapeDtypeStruct(array.shape, array.dtype),
        in_specs=[ANY],
        out_specs=ANY,
        scratch_shapes=[pltpu.SemaphoreType.DMA] * 3,
        compiler_params=pltpu.CompilerParams(collective_id=collective_id, has_side_effects=True),
        name=f"swap_{collective_id}",
    )(array)


def share_kernel(src, dst, send_sem, recv_sem, own_sem):
    y = lax.axis_index("y")
    up, down = (y + 1) % 4, (y + 3) % 4
    own = pltpu.make_async_copy(src, dst.at[:, y], own_sem)
    own.start()
    barrier = pltpu.get_barrier_semaphore()
    for target in (up, down):
        pl.semaphore_signal(barrier, inc=1, device_id={"y": target}, device_id_type=BY_MESH)
    pl.semaphore_wait(barrier, 2)

    def send(block, slot, c, target, lane):
        copy = pltpu.make_async_remote_copy(
            src_ref=block,
            dst_ref=dst.at[:, slot, c],
            send_sem=send_sem.at[lane, c],
            recv_sem=recv_sem.at[lane, c],
            device_id={"y": target},
            device_id_type=BY_MESH,
        )
        copy.start()
        return copy

    ups, downs, far = {}, {}, []
    for step in range(4):
        c, d = step, (step + 2) % 4
        ups[c] = send(src.at[:, c], y, c, up, 0)
        downs[d] = send(src.at[:, d], y, d, down, 1)
    for step in range(2):
        c, d = step, step + 2
        ups[c].wait_recv()
        far.append(send(dst.at[:, down, c], down, c, up, 2))
        downs[d].wait_recv()
        far.append(send(dst.at[:, up, d], up, d, down, 2))
    for step in range(2):
        ups[step + 2].wait_recv()
        downs[step].wait_recv()
    for copy in far:
        copy.wait_recv()
    for copy in (*ups.values(), *downs.values(), *far):
        copy.wait_send()
    own.wait()


def share(grads):
    m, c, f, k = grads.shape
    return pl.pallas_call(
        share_kernel,
        out_shape=jax.ShapeDtypeStruct((m, 4, c, f, k), grads.dtype),
        in_specs=[ANY],
        out_specs=ANY,
        scratch_shapes=[
            pltpu.SemaphoreType.DMA((3, 4)),
            pltpu.SemaphoreType.DMA((3, 4)),
            pltpu.SemaphoreType.DMA,
        ],
        compiler_params=pltpu.CompilerParams(collective_id=3, has_side_effects=True),
        name="share",
    )(grads)


def deliver_kernel(part, dst, other, total, core_send, core_recv, send_sem, recv_sem, own_sem):
    z, y, x = position()
    zl, core = lax.axis_index("zl"), lax.axis_index("c")
    slot = ((y * 4 + z) * 4 + x) * 2 + zl
    barrier = pltpu.get_barrier_semaphore()

    def peer(step):
        return {
            "z": (z + step // 16) % 4,
            "y": (y + (step // 4) % 4) % 4,
            "x": (x + step % 4) % 4,
        }

    def greet(first, half):
        def body(step, carry):
            pl.semaphore_signal(
                barrier, inc=1, device_id={**peer(step), "zl": half}, device_id_type=BY_MESH
            )
            return carry

        lax.fori_loop(first, 64, body, 0)

    pl.semaphore_signal(barrier, inc=1, device_id={"c": 1 - core}, device_id_type=BY_MESH)
    greet(0, 1 - zl)
    greet(1, zl)
    pl.semaphore_wait(barrier, 128)

    halves = (1 - zl, zl)
    copies = []
    for at, half in enumerate(halves):
        copy = pltpu.make_async_remote_copy(
            src_ref=part.at[2 * half + 1 - core],
            dst_ref=other.at[at],
            send_sem=core_send.at[at],
            recv_sem=core_recv.at[at],
            device_id={"c": 1 - core},
            device_id_type=BY_MESH,
        )
        copy.start()
        copies.append(copy)
    for at, half in enumerate(halves):
        copies[at].wait_recv()
        both = part[2 * half + core].astype(F32) + other[at].astype(F32)
        total[at] = pltpu.einshape("abk->bak", both.reshape(16, 64, 256)).astype(BF16)

        def send(step, carry):
            to = peer(step)
            pltpu.make_async_remote_copy(
                src_ref=total.at[at, to["z"] * 16 + to["y"] * 4 + to["x"]],
                dst_ref=dst.at[slot],
                send_sem=send_sem,
                recv_sem=recv_sem,
                device_id={**to, "zl": half},
                device_id_type=BY_MESH,
            ).start()
            return carry

        lax.fori_loop(at, 64, send, 0)
    own = pltpu.make_async_copy(total.at[1, z * 16 + y * 4 + x], dst.at[slot], own_sem)
    own.start()
    most = dst.at[pl.ds(0, 127)]
    pltpu.make_async_copy(most, most, send_sem).wait()
    pltpu.make_async_copy(most, most, recv_sem).wait()
    for copy in copies:
        copy.wait_send()
    own.wait()


def deliver(part):
    return pl.pallas_call(
        deliver_kernel,
        out_shape=jax.ShapeDtypeStruct((128, 16, 256), part.dtype),
        in_specs=[pl.BlockSpec(memory_space=pltpu.VMEM)],
        out_specs=ANY,
        scratch_shapes=[
            pltpu.VMEM((2, 1024, 256), part.dtype),
            pltpu.VMEM((2, 64, 16, 256), part.dtype),
            pltpu.SemaphoreType.DMA((2,)),
            pltpu.SemaphoreType.DMA((2,)),
            pltpu.SemaphoreType.DMA,
            pltpu.SemaphoreType.DMA,
            pltpu.SemaphoreType.DMA,
        ],
        compiler_params=pltpu.CompilerParams(
            collective_id=2, has_side_effects=True, vmem_limit_bytes=24 << 20
        ),
        name="deliver",
    )(part)


def patch_order():
    z, x, _, slot, c = np.indices((4, 4, 2, 4, 4)).reshape(5, 512)
    return np.eye(256, dtype=np.float32)[4 * (z * 16 + slot * 4 + x) + c]


def temporal(q_heads, k_heads, v_heads, g_heads):
    scale = 1.0 / q_heads.shape[-1] ** 0.5
    scores = (
        jnp.einsum("fphd,gphd->phfg", q_heads, k_heads, preferred_element_type=F32) * scale
    )
    probs = jax.nn.softmax(scores, axis=-1)
    probs_b = probs.astype(BF16)
    attended = jnp.einsum("phfg,gphd->fphd", probs_b, v_heads, preferred_element_type=F32)
    delta = jnp.transpose(jnp.sum(g_heads.astype(F32) * attended, axis=-1), (1, 2, 0))
    grad_probs = jnp.einsum("fphd,gphd->phfg", g_heads, v_heads, preferred_element_type=F32)
    grad_scores = (probs * (grad_probs - delta[..., None])).astype(BF16)
    grad_value = jnp.einsum("phfg,fphd->pghd", probs_b, g_heads, preferred_element_type=F32)
    grad_query = (
        jnp.einsum("phfg,gphd->pfhd", grad_scores, k_heads, preferred_element_type=F32) * scale
    )
    grad_key = (
        jnp.einsum("phfg,fphd->pghd", grad_scores, q_heads, preferred_element_type=F32) * scale
    )
    return grad_query.astype(BF16), grad_key.astype(BF16), grad_value.astype(BF16)


def per_device(query, key_in, value, grad_out, weights):
    rows = lax.all_gather(weights, ("z", "x"), axis=1, tiled=True)
    packed = jnp.stack([a.reshape(64, 4, 1024) for a in (query, key_in, value, grad_out)], axis=1)
    moved = swap(packed.reshape(64, 16, 1024), 1).reshape(64, 4, 4, 8, HD)
    grads = temporal(moved[:, 0], moved[:, 1], moved[:, 2], moved[:, 3])
    stacked = jnp.stack([a.reshape(4, 64, 1024) for a in grads])
    shared = share(stacked).reshape(3, 1024, 1024)
    partial_sum = jnp.einsum(
        "mtk,mzik->zti", shared, rows.reshape(3, 4, 256, 1024), preferred_element_type=F32
    ).astype(BF16)
    back = deliver(partial_sum).reshape(4, 512, 256)
    place = jnp.asarray(patch_order(), BF16)
    out = jnp.einsum("ytk,tp->ykp", back, place, preferred_element_type=F32)
    return out.reshape(1024, 256).astype(BF16)


def solution(mesh):
    fine = Mesh(mesh.devices.reshape(4, 4, 4, 2, 2), AXES)
    placed = (P(TM, HEAD),) * 4 + (P(None, TM, HEAD),)
    return jax.shard_map(
        per_device, mesh=fine, in_specs=placed, out_specs=P(HEAD, TM), check_vma=False
    )
```

```python
import jax
import jax.numpy as jnp
import numpy as np
from jax import lax
from jax.experimental import pallas as pl
from jax.experimental.pallas import tpu as pltpu
from jax.sharding import Mesh, PartitionSpec as P

HD = 128
AXES = ("z", "y", "x", "zl", "c")
TM = AXES[:3]
HEAD = AXES[3:]
BF16 = jnp.bfloat16
F32 = jnp.float32
BY_MESH = pl.DeviceIdType.MESH
ANY = pl.BlockSpec(memory_space=pl.ANY)


def position():
    return lax.axis_index("z"), lax.axis_index("y"), lax.axis_index("x")


def tm_peer(place, step):
    z, y, x = place
    return {
        "z": (z + step // 16) % 4,
        "y": (y + (step // 4) % 4) % 4,
        "x": (x + step % 4) % 4,
    }


def tm_index(at):
    return at["z"] * 16 + at["y"] * 4 + at["x"]


def greet_all(place):
    barrier = pltpu.get_barrier_semaphore()

    def greet(step, carry):
        pl.semaphore_signal(
            barrier, inc=1, device_id=tm_peer(place, step), device_id_type=BY_MESH
        )
        return carry

    lax.fori_loop(1, 64, greet, 0)
    pl.semaphore_wait(barrier, 63)


def swap_start(place, src, dst, send_sem, recv_sem, own_sem):
    me = tm_index(tm_peer(place, 0))
    own = pltpu.make_async_copy(src.at[me], dst.at[me], own_sem)
    own.start()

    def send(step, carry):
        to = tm_peer(place, step)
        pltpu.make_async_remote_copy(
            src_ref=src.at[tm_index(to)],
            dst_ref=dst.at[me],
            send_sem=send_sem,
            recv_sem=recv_sem,
            device_id=to,
            device_id_type=BY_MESH,
        ).start()
        return carry

    lax.fori_loop(1, 64, send, 0)
    return own


def swap_wait(own, src, dst, send_sem, recv_sem):
    most = pl.ds(0, 63)
    pltpu.make_async_copy(src.at[most], src.at[most], send_sem).wait()
    pltpu.make_async_copy(dst.at[most], dst.at[most], recv_sem).wait()
    own.wait()


def share_start(y, src, dst, send_sem, recv_sem, own_sem):
    up, down = (y + 1) % 4, (y + 3) % 4
    own = pltpu.make_async_copy(src, dst.at[:, y], own_sem)
    own.start()

    def send(block, slot, c, target, lane):
        copy = pltpu.make_async_remote_copy(
            src_ref=block,
            dst_ref=dst.at[:, slot, c],
            send_sem=send_sem.at[lane, c],
            recv_sem=recv_sem.at[lane, c],
            device_id={"y": target},
            device_id_type=BY_MESH,
        )
        copy.start()
        return copy

    ups, downs = {}, {}
    for step in range(4):
        c, d = step, (step + 2) % 4
        ups[c] = send(src.at[:, c], y, c, up, 0)
        downs[d] = send(src.at[:, d], y, d, down, 1)

    def finish():
        far = []
        for step in range(2):
            c, d = step, step + 2
            ups[c].wait_recv()
            far.append(send(dst.at[:, down, c], down, c, up, 2))
            downs[d].wait_recv()
            far.append(send(dst.at[:, up, d], up, d, down, 2))
        for step in range(2):
            ups[step + 2].wait_recv()
            downs[step].wait_recv()
        for copy in far:
            copy.wait_recv()
        for copy in (*ups.values(), *downs.values(), *far):
            copy.wait_send()
        own.wait()

    return finish


def first_kernel(query, key_in, value, grad_out, moved, later, packed, *swap_sems):
    place = position()
    width = moved.shape[-1]
    greet_all(place)
    row = lax.broadcasted_iota(jnp.int32, (64, 64), 0)
    column = lax.broadcasted_iota(jnp.int32, (64, 64), 1)
    wanted = ((row // 4) % 4) * 16 + (row // 16) * 4 + row % 4
    order = jnp.where(column == wanted, 1.0, 0.0).astype(BF16)

    def pack(into, columns):
        def body(group, carry):
            rows = pl.ds(pl.multiple_of(group * 16, 16), 16)
            block = jnp.concatenate(
                [ref[rows, columns] for ref in (query, key_in, value, grad_out)], axis=0
            )
            ordered = jnp.dot(order, block, preferred_element_type=F32).astype(BF16)
            into[pl.ds(group * 4, 4)] = ordered.reshape(4, 16, width)
            return carry

        lax.fori_loop(0, 16, body, 0)

    pack(packed, pl.ds(0, width))
    own = swap_start(place, packed, moved, *swap_sems)
    pack(later, pl.ds(width, width))
    swap_wait(own, packed, moved, *swap_sems[:2])


def second_kernel(src, grads, moved, shared, *sems):
    place = position()
    greet_all(place)
    finish = share_start(place[1], grads, shared, *sems[3:])
    own = swap_start(place, src, moved, *sems[:3])
    finish()
    swap_wait(own, src, moved, *sems[:2])


def third_kernel(grads, shared, *sems):
    y = lax.axis_index("y")
    barrier = pltpu.get_barrier_semaphore()
    for step in (1, 3):
        pl.semaphore_signal(barrier, inc=1, device_id={"y": (y + step) % 4}, device_id_type=BY_MESH)
    pl.semaphore_wait(barrier, 2)
    share_start(y, grads, shared, *sems)()


SWAP_SEMS = [pltpu.SemaphoreType.DMA] * 3
SHARE_SEMS = [
    pltpu.SemaphoreType.DMA((3, 4)),
    pltpu.SemaphoreType.DMA((3, 4)),
    pltpu.SemaphoreType.DMA,
]
VMEM = pl.BlockSpec(memory_space=pltpu.VMEM)


def params(collective_id):
    return pltpu.CompilerParams(
        collective_id=collective_id, has_side_effects=True, vmem_limit_bytes=24 << 20
    )


def first(*arrays):
    block = jax.ShapeDtypeStruct((64, 16, 512), BF16)
    return pl.pallas_call(
        first_kernel,
        out_shape=(block, block),
        in_specs=[VMEM] * 4,
        out_specs=(ANY, VMEM),
        scratch_shapes=[pltpu.VMEM(block.shape, BF16), *SWAP_SEMS],
        compiler_params=params(1),
        name="swap_first",
    )(*arrays)


def second(src, grads):
    return pl.pallas_call(
        second_kernel,
        out_shape=(
            jax.ShapeDtypeStruct(src.shape, BF16),
            jax.ShapeDtypeStruct((3, 4, 4, 64, 512), BF16),
        ),
        in_specs=[ANY, ANY],
        out_specs=(ANY, ANY),
        scratch_shapes=[*SWAP_SEMS, *SHARE_SEMS],
        compiler_params=params(3),
        name="swap_and_share",
    )(src, grads)


def third(grads):
    return pl.pallas_call(
        third_kernel,
        out_shape=jax.ShapeDtypeStruct((3, 4, 4, 64, 512), BF16),
        in_specs=[ANY],
        out_specs=ANY,
        scratch_shapes=SHARE_SEMS,
        compiler_params=params(4),
        name="share_last",
    )(grads)


def deliver_kernel(part, dst, other, total, core_send, core_recv, send_sem, recv_sem, own_sem):
    z, y, x = position()
    zl, core = lax.axis_index("zl"), lax.axis_index("c")
    slot = ((y * 4 + z) * 4 + x) * 2 + zl
    barrier = pltpu.get_barrier_semaphore()

    def peer(step):
        return tm_peer((z, y, x), step)

    def greet(first, half):
        def body(step, carry):
            pl.semaphore_signal(
                barrier, inc=1, device_id={**peer(step), "zl": half}, device_id_type=BY_MESH
            )
            return carry

        lax.fori_loop(first, 64, body, 0)

    pl.semaphore_signal(barrier, inc=1, device_id={"c": 1 - core}, device_id_type=BY_MESH)
    greet(0, 1 - zl)
    greet(1, zl)
    pl.semaphore_wait(barrier, 128)

    halves = (1 - zl, zl)
    copies = []
    for at, half in enumerate(halves):
        copy = pltpu.make_async_remote_copy(
            src_ref=part.at[2 * half + 1 - core],
            dst_ref=other.at[at],
            send_sem=core_send.at[at],
            recv_sem=core_recv.at[at],
            device_id={"c": 1 - core},
            device_id_type=BY_MESH,
        )
        copy.start()
        copies.append(copy)
    for at, half in enumerate(halves):
        copies[at].wait_recv()
        both = part[2 * half + core].astype(F32) + other[at].astype(F32)
        total[at] = pltpu.einshape("abk->bak", both.reshape(16, 64, 256)).astype(BF16)

        def send(step, carry):
            to = peer(step)
            pltpu.make_async_remote_copy(
                src_ref=total.at[at, tm_index(to)],
                dst_ref=dst.at[slot],
                send_sem=send_sem,
                recv_sem=recv_sem,
                device_id={**to, "zl": half},
                device_id_type=BY_MESH,
            ).start()
            return carry

        lax.fori_loop(at, 64, send, 0)
    own = pltpu.make_async_copy(total.at[1, z * 16 + y * 4 + x], dst.at[slot], own_sem)
    own.start()
    most = dst.at[pl.ds(0, 127)]
    pltpu.make_async_copy(most, most, send_sem).wait()
    pltpu.make_async_copy(most, most, recv_sem).wait()
    for copy in copies:
        copy.wait_send()
    own.wait()


def deliver(part):
    return pl.pallas_call(
        deliver_kernel,
        out_shape=jax.ShapeDtypeStruct((128, 16, 256), part.dtype),
        in_specs=[pl.BlockSpec(memory_space=pltpu.VMEM)],
        out_specs=ANY,
        scratch_shapes=[
            pltpu.VMEM((2, 1024, 256), part.dtype),
            pltpu.VMEM((2, 64, 16, 256), part.dtype),
            pltpu.SemaphoreType.DMA((2,)),
            pltpu.SemaphoreType.DMA((2,)),
            pltpu.SemaphoreType.DMA,
            pltpu.SemaphoreType.DMA,
            pltpu.SemaphoreType.DMA,
        ],
        compiler_params=params(2),
        name="deliver",
    )(part)


def patch_order():
    z, x, _, slot, c = np.indices((4, 4, 2, 4, 4)).reshape(5, 512)
    return np.eye(256, dtype=np.float32)[4 * (z * 16 + slot * 4 + x) + c]


def temporal(q_heads, k_heads, v_heads, g_heads):
    scale = 1.0 / q_heads.shape[-1] ** 0.5
    scores = (
        jnp.einsum("fphd,gphd->phfg", q_heads, k_heads, preferred_element_type=F32) * scale
    )
    probs = jax.nn.softmax(scores, axis=-1)
    probs_b = probs.astype(BF16)
    attended = jnp.einsum("phfg,gphd->fphd", probs_b, v_heads, preferred_element_type=F32)
    delta = jnp.transpose(jnp.sum(g_heads.astype(F32) * attended, axis=-1), (1, 2, 0))
    grad_probs = jnp.einsum("fphd,gphd->phfg", g_heads, v_heads, preferred_element_type=F32)
    grad_scores = (probs * (grad_probs - delta[..., None])).astype(BF16)
    grad_value = jnp.einsum("phfg,fphd->pghd", probs_b, g_heads, preferred_element_type=F32)
    grad_query = (
        jnp.einsum("phfg,gphd->pfhd", grad_scores, k_heads, preferred_element_type=F32) * scale
    )
    grad_key = (
        jnp.einsum("phfg,fphd->pghd", grad_scores, q_heads, preferred_element_type=F32) * scale
    )
    return grad_query.astype(BF16), grad_key.astype(BF16), grad_value.astype(BF16)


def gradients(moved):
    moved = moved.reshape(64, 4, 4, 4, HD)
    grads = temporal(moved[:, 0], moved[:, 1], moved[:, 2], moved[:, 3])
    return jnp.stack([a.reshape(4, 64, 512) for a in grads])


def product(shared, rows):
    return jnp.einsum(
        "mtk,mzik->zti",
        shared.reshape(3, 1024, 512),
        rows.reshape(3, 4, 256, 512),
        preferred_element_type=F32,
    )


def per_device(query, key_in, value, grad_out, weights):
    rows = [
        lax.all_gather(weights[:, :, at : at + 512], ("z", "x"), axis=1, tiled=True)
        for at in (0, 512)
    ]
    moved, later = first(query, key_in, value, grad_out)
    moved, shared = second(later, gradients(moved))
    grads = gradients(moved)
    partial_sum = product(shared, rows[0]) + product(third(grads), rows[1])
    back = deliver(partial_sum.astype(BF16)).reshape(4, 512, 256)
    place = jnp.asarray(patch_order(), BF16)
    out = jnp.einsum("ytk,tp->ykp", back, place, preferred_element_type=F32)
    return out.reshape(1024, 256).astype(BF16)


def solution(mesh):
    fine = Mesh(mesh.devices.reshape(4, 4, 4, 2, 2), AXES)
    placed = (P(TM, HEAD),) * 4 + (P(None, TM, HEAD),)
    return jax.shard_map(
        per_device, mesh=fine, in_specs=placed, out_specs=P(HEAD, TM), check_vma=False
    )
```

```python
import jax
import jax.numpy as jnp
import numpy as np
from jax import lax
from jax.experimental import pallas as pl
from jax.experimental.pallas import tpu as pltpu
from jax.sharding import Mesh, PartitionSpec as P

HD = 128
WIDTH = 512
AXES = ("z", "y", "x", "zl", "c")
TM = AXES[:3]
HEAD = AXES[3:]
BF16 = jnp.bfloat16
F32 = jnp.float32
BY_MESH = pl.DeviceIdType.MESH
ANY = pl.BlockSpec(memory_space=pl.ANY)


def position():
    return lax.axis_index("z"), lax.axis_index("y"), lax.axis_index("x")


def tm_peer(place, step):
    z, y, x = place
    return {
        "z": (z + step // 16) % 4,
        "y": (y + (step // 4) % 4) % 4,
        "x": (x + step % 4) % 4,
    }


def tm_index(at):
    return at["z"] * 16 + at["y"] * 4 + at["x"]


def greet_all(place):
    barrier = pltpu.get_barrier_semaphore()

    def greet(step, carry):
        pl.semaphore_signal(
            barrier, inc=1, device_id=tm_peer(place, step), device_id_type=BY_MESH
        )
        return carry

    lax.fori_loop(1, 64, greet, 0)
    pl.semaphore_wait(barrier, 63)


def swap_start(place, src, dst, send_sem, recv_sem, own_sem):
    me = tm_index(tm_peer(place, 0))
    own = pltpu.make_async_copy(src.at[me], dst.at[me], own_sem)
    own.start()

    def send(step, carry):
        to = tm_peer(place, step)
        pltpu.make_async_remote_copy(
            src_ref=src.at[tm_index(to)],
            dst_ref=dst.at[me],
            send_sem=send_sem,
            recv_sem=recv_sem,
            device_id=to,
            device_id_type=BY_MESH,
        ).start()
        return carry

    lax.fori_loop(1, 64, send, 0)
    return own


def swap_wait(own, src, dst, send_sem, recv_sem):
    most = pl.ds(0, 63)
    pltpu.make_async_copy(src.at[most], src.at[most], send_sem).wait()
    pltpu.make_async_copy(dst.at[most], dst.at[most], recv_sem).wait()
    own.wait()


def share_start(y, src, dst, columns, send_sem, recv_sem, own_sem):
    up, down = (y + 1) % 4, (y + 3) % 4
    own = pltpu.make_async_copy(
        src.at[:, :, :, columns], dst.at[:, y, :, :, columns], own_sem
    )
    own.start()

    def send(block, slot, c, target, lane):
        copy = pltpu.make_async_remote_copy(
            src_ref=block,
            dst_ref=dst.at[:, slot, c, :, columns],
            send_sem=send_sem.at[lane, c],
            recv_sem=recv_sem.at[lane, c],
            device_id={"y": target},
            device_id_type=BY_MESH,
        )
        copy.start()
        return copy

    ups, downs = {}, {}
    for step in range(4):
        c, d = step, (step + 2) % 4
        ups[c] = send(src.at[:, c, :, columns], y, c, up, 0)
        downs[d] = send(src.at[:, d, :, columns], y, d, down, 1)

    far = []

    def forward():
        for step in range(2):
            c, d = step, step + 2
            ups[c].wait_recv()
            far.append(send(dst.at[:, down, c, :, columns], down, c, up, 2))
            downs[d].wait_recv()
            far.append(send(dst.at[:, up, d, :, columns], up, d, down, 2))

    def finish():
        for step in range(2):
            ups[step + 2].wait_recv()
            downs[step].wait_recv()
        for copy in far:
            copy.wait_recv()
        for copy in (*ups.values(), *downs.values(), *far):
            copy.wait_send()
        own.wait()

    return forward, finish


def pack(arrays, into, columns):
    row = lax.broadcasted_iota(jnp.int32, (64, 64), 0)
    column = lax.broadcasted_iota(jnp.int32, (64, 64), 1)
    wanted = ((row // 4) % 4) * 16 + (row // 16) * 4 + row % 4
    order = jnp.where(column == wanted, 1.0, 0.0).astype(BF16)

    def body(group, carry):
        rows = pl.ds(pl.multiple_of(group * 16, 16), 16)
        block = jnp.concatenate([ref[rows, columns] for ref in arrays], axis=0)
        ordered = jnp.dot(order, block, preferred_element_type=F32).astype(BF16)
        into[pl.ds(group * 4, 4)] = ordered.reshape(4, 16, WIDTH)
        return carry

    lax.fori_loop(0, 16, body, 0)


def attend(moved, heads, grads, chunk):
    heads[...] = pltpu.einshape("abk->bak", moved[...].astype(F32)).astype(BF16)
    scale = 1.0 / HD**0.5
    row = lax.broadcasted_iota(jnp.int32, (128, 128), 0)
    column = lax.broadcasted_iota(jnp.int32, (128, 128), 1)
    same = row // 64 == column // 64

    def dot(a, b, over_a, over_b):
        return lax.dot_general(
            a, b, (((over_a,), (over_b,)), ((), ())), preferred_element_type=F32
        )

    def body(pair, carry):
        patches = pl.ds(pair * 2, 2)
        for head in range(WIDTH // HD):
            lanes = slice(head * HD, (head + 1) * HD)
            q, k, v, g = (
                heads[pl.ds(array * 4 + pair * 2, 2), :, lanes].reshape(128, HD)
                for array in range(4)
            )
            scores = jnp.where(same, dot(q, k, 1, 1) * scale, -1e30)
            weight = jnp.exp(scores - jnp.max(scores, axis=1, keepdims=True))
            probs = weight / jnp.sum(weight, axis=1, keepdims=True)
            probs_b = probs.astype(BF16)
            attended = dot(probs_b, v, 1, 0)
            delta = jnp.sum(g.astype(F32) * attended, axis=1, keepdims=True)
            grad_scores = (probs * (dot(g, v, 1, 1) - delta)).astype(BF16)
            results = (
                dot(grad_scores, k, 1, 0) * scale,
                dot(grad_scores, q, 0, 0) * scale,
                dot(probs_b, g, 0, 0),
            )
            out = pl.ds(chunk * WIDTH + head * HD, HD)
            for m, result in enumerate(results):
                grads[m, patches, :, out] = result.astype(BF16).reshape(2, 64, HD)
        return carry

    lax.fori_loop(0, 2, body, 0)


def rows_start(place, own_rows, rows, send_sem, recv_sem, own_sem):
    z, y, x = place
    steps = (0, 3, 2, 1)

    def block(b, at_x, part=slice(None)):
        return rows.at[:, ((z + steps[b]) % 4) * 4 + at_x, part]

    def send(src, dst, axis, target, lane, b):
        copy = pltpu.make_async_remote_copy(
            src_ref=src,
            dst_ref=dst,
            send_sem=send_sem.at[lane, b],
            recv_sem=recv_sem.at[lane, b],
            device_id={axis: target},
            device_id_type=BY_MESH,
        )
        copy.start()
        return copy

    z_up, z_down, x_up, x_down = (z + 1) % 4, (z + 3) % 4, (x + 1) % 4, (x + 3) % 4
    own = pltpu.make_async_copy(own_rows, block(0, x), own_sem)
    own.start()
    z_ups = send(own_rows, block(0, x), "z", z_up, 0, 0)
    z_downs = send(own_rows, block(0, x), "z", z_down, 0, 1)
    z_far, ups, downs, far = [], {}, {}, {}

    def along_x(b):
        src = own_rows if b == 0 else block(b, x)
        ups[b] = send(src, block(b, x), "x", x_up, 1, b)
        downs[b] = send(src, block(b, x), "x", x_down, 2, b)

    along_x(0)

    def near():
        low, high = pl.ds(0, 32), pl.ds(32, 32)
        z_ups.wait_recv()
        z_far.append(send(block(1, x, low), block(1, x, low), "z", z_up, 0, 2))
        along_x(1)
        z_downs.wait_recv()
        z_far.append(send(block(3, x, high), block(3, x, high), "z", z_down, 0, 3))
        along_x(3)

    def across():
        for copy in z_far:
            copy.wait_recv()
        along_x(2)

    def forward(b):
        if b < 2:
            ups[b].wait_recv()
            far[b] = send(block(b, x_down), block(b, x_down), "x", x_up, 3, b)
        else:
            downs[b].wait_recv()
            far[b] = send(block(b, x_up), block(b, x_up), "x", x_down, 3, b)

    def finish():
        for b in range(4):
            (downs if b < 2 else ups)[b].wait_recv()
            far[b].wait_recv()
        for copy in (z_ups, z_downs, *z_far, *ups.values(), *downs.values(), *far.values()):
            copy.wait_send()
        own.wait()

    return near, across, forward, finish


def front_kernel(
    query, key_in, value, grad_out, own_rows, shared, rows, packed, moved, heads, grads, *sems
):
    place = position()
    arrays = (query, key_in, value, grad_out)
    swap_sems, share_sems, rows_sems = (sems[:3], sems[3:6]), (sems[6:9], sems[9:12]), sems[12:]
    greet_all(place)
    near, across, pass_on, rows_finish = rows_start(place, own_rows, rows, *rows_sems)
    swaps = []
    for chunk in range(2):
        pack(arrays, packed.at[chunk], pl.ds(chunk * WIDTH, WIDTH))
        swaps.append(swap_start(place, packed.at[chunk], moved.at[chunk], *swap_sems[chunk]))

    def swapped(chunk):
        swap_wait(swaps[chunk], packed.at[chunk], moved.at[chunk], *swap_sems[chunk][:2])
        attend(moved.at[chunk], heads, grads, chunk)
        columns = pl.ds(chunk * WIDTH, WIDTH)
        return share_start(place[1], grads, shared, columns, *share_sems[chunk])

    near()
    forward, share_finish = swapped(0)
    pass_on(0)
    across()
    forward()
    pass_on(1)
    pass_on(3)
    last_forward, last_finish = swapped(1)
    pass_on(2)
    last_forward()
    share_finish()
    last_finish()
    rows_finish()


SWAP_SEMS = [pltpu.SemaphoreType.DMA] * 3
SHARE_SEMS = [
    pltpu.SemaphoreType.DMA((3, 4)),
    pltpu.SemaphoreType.DMA((3, 4)),
    pltpu.SemaphoreType.DMA,
]
ROWS_SEMS = [
    pltpu.SemaphoreType.DMA((4, 4)),
    pltpu.SemaphoreType.DMA((4, 4)),
    pltpu.SemaphoreType.DMA,
]
VMEM = pl.BlockSpec(memory_space=pltpu.VMEM)


def params(collective_id):
    return pltpu.CompilerParams(
        collective_id=collective_id, has_side_effects=True, vmem_limit_bytes=32 << 20
    )


def front(*arrays):
    return pl.pallas_call(
        front_kernel,
        out_shape=(
            jax.ShapeDtypeStruct((3, 4, 4, 64, 2 * WIDTH), BF16),
            jax.ShapeDtypeStruct((3, 16, 64, 2 * WIDTH), BF16),
        ),
        in_specs=[VMEM] * 4 + [ANY],
        out_specs=(ANY, ANY),
        scratch_shapes=[
            pltpu.VMEM((2, 64, 16, WIDTH), BF16),
            pltpu.VMEM((2, 64, 16, WIDTH), BF16),
            pltpu.VMEM((16, 64, WIDTH), BF16),
            pltpu.VMEM((3, 4, 64, 2 * WIDTH), BF16),
            *SWAP_SEMS,
            *SWAP_SEMS,
            *SHARE_SEMS,
            *SHARE_SEMS,
            *ROWS_SEMS,
        ],
        compiler_params=params(1),
        name="front",
    )(*arrays)


def deliver_kernel(part, dst, other, total, core_send, core_recv, send_sem, recv_sem, own_sem):
    z, y, x = position()
    zl, core = lax.axis_index("zl"), lax.axis_index("c")
    slot = ((y * 4 + z) * 4 + x) * 2 + zl
    barrier = pltpu.get_barrier_semaphore()

    def peer(step):
        return tm_peer((z, y, x), step)

    def greet(first, half):
        def body(step, carry):
            pl.semaphore_signal(
                barrier, inc=1, device_id={**peer(step), "zl": half}, device_id_type=BY_MESH
            )
            return carry

        lax.fori_loop(first, 64, body, 0)

    pl.semaphore_signal(barrier, inc=1, device_id={"c": 1 - core}, device_id_type=BY_MESH)
    greet(0, 1 - zl)
    greet(1, zl)
    pl.semaphore_wait(barrier, 128)

    halves = (1 - zl, zl)
    copies = []
    for at, half in enumerate(halves):
        copy = pltpu.make_async_remote_copy(
            src_ref=part.at[2 * half + 1 - core],
            dst_ref=other.at[at],
            send_sem=core_send.at[at],
            recv_sem=core_recv.at[at],
            device_id={"c": 1 - core},
            device_id_type=BY_MESH,
        )
        copy.start()
        copies.append(copy)
    for at, half in enumerate(halves):
        copies[at].wait_recv()
        both = part[2 * half + core].astype(F32) + other[at].astype(F32)
        total[at] = pltpu.einshape("abk->bak", both.reshape(16, 64, 256)).astype(BF16)

        def send(step, carry):
            to = peer(step)
            pltpu.make_async_remote_copy(
                src_ref=total.at[at, tm_index(to)],
                dst_ref=dst.at[slot],
                send_sem=send_sem,
                recv_sem=recv_sem,
                device_id={**to, "zl": half},
                device_id_type=BY_MESH,
            ).start()
            return carry

        lax.fori_loop(at, 64, send, 0)
    own = pltpu.make_async_copy(total.at[1, z * 16 + y * 4 + x], dst.at[slot], own_sem)
    own.start()
    most = dst.at[pl.ds(0, 127)]
    pltpu.make_async_copy(most, most, send_sem).wait()
    pltpu.make_async_copy(most, most, recv_sem).wait()
    for copy in copies:
        copy.wait_send()
    own.wait()


def deliver(part):
    return pl.pallas_call(
        deliver_kernel,
        out_shape=jax.ShapeDtypeStruct((128, 16, 256), part.dtype),
        in_specs=[pl.BlockSpec(memory_space=pltpu.VMEM)],
        out_specs=ANY,
        scratch_shapes=[
            pltpu.VMEM((2, 1024, 256), part.dtype),
            pltpu.VMEM((2, 64, 16, 256), part.dtype),
            pltpu.SemaphoreType.DMA((2,)),
            pltpu.SemaphoreType.DMA((2,)),
            pltpu.SemaphoreType.DMA,
            pltpu.SemaphoreType.DMA,
            pltpu.SemaphoreType.DMA,
        ],
        compiler_params=params(2),
        name="deliver",
    )(part)


def patch_order():
    z, x, _, slot, c = np.indices((4, 4, 2, 4, 4)).reshape(5, 512)
    return np.eye(256, dtype=np.float32)[4 * (z * 16 + slot * 4 + x) + c]


def per_device(query, key_in, value, grad_out, weights):
    shared, rows = front(query, key_in, value, grad_out, weights)
    partial_sum = jnp.einsum(
        "mtk,mzik->zti",
        shared.reshape(3, 1024, 1024),
        rows.reshape(3, 4, 256, 1024),
        preferred_element_type=F32,
    )
    back = deliver(partial_sum.astype(BF16)).reshape(4, 512, 256)
    place = jnp.asarray(patch_order(), BF16)
    out = jnp.einsum("ytk,tp->ykp", back, place, preferred_element_type=F32)
    return out.reshape(1024, 256).astype(BF16)


def solution(mesh):
    fine = Mesh(mesh.devices.reshape(4, 4, 4, 2, 2), AXES)
    placed = (P(TM, HEAD),) * 4 + (P(None, TM, HEAD),)
    return jax.shard_map(
        per_device, mesh=fine, in_specs=placed, out_specs=P(HEAD, TM), check_vma=False
    )
```

```python
import jax
import jax.numpy as jnp
import numpy as np
from jax import lax
from jax.experimental import pallas as pl
from jax.experimental.pallas import tpu as pltpu
from jax.sharding import Mesh, PartitionSpec as P

HD = 128
CHUNKS = 4
WIDTH = 1024 // CHUNKS
AXES = ("z", "y", "x", "zl", "c")
TM = AXES[:3]
HEAD = AXES[3:]
BF16 = jnp.bfloat16
F32 = jnp.float32
BY_MESH = pl.DeviceIdType.MESH
ANY = pl.BlockSpec(memory_space=pl.ANY)


def position():
    return lax.axis_index("z"), lax.axis_index("y"), lax.axis_index("x")


def tm_peer(place, step):
    z, y, x = place
    return {
        "z": (z + step // 16) % 4,
        "y": (y + (step // 4) % 4) % 4,
        "x": (x + step % 4) % 4,
    }


def tm_index(at):
    return at["z"] * 16 + at["y"] * 4 + at["x"]


def greet_all(place):
    barrier = pltpu.get_barrier_semaphore()

    def greet(step, carry):
        pl.semaphore_signal(
            barrier, inc=1, device_id=tm_peer(place, step), device_id_type=BY_MESH
        )
        return carry

    lax.fori_loop(1, 64, greet, 0)
    pl.semaphore_wait(barrier, 63)


def swap_start(place, src, dst, send_sem, recv_sem, own_sem):
    me = tm_index(tm_peer(place, 0))
    own = pltpu.make_async_copy(src.at[me], dst.at[me], own_sem)
    own.start()

    def send(step, carry):
        to = tm_peer(place, step)
        pltpu.make_async_remote_copy(
            src_ref=src.at[tm_index(to)],
            dst_ref=dst.at[me],
            send_sem=send_sem,
            recv_sem=recv_sem,
            device_id=to,
            device_id_type=BY_MESH,
        ).start()
        return carry

    lax.fori_loop(1, 64, send, 0)
    return own


def swap_wait(own, src, dst, send_sem, recv_sem):
    most = pl.ds(0, 63)
    pltpu.make_async_copy(src.at[most], src.at[most], send_sem).wait()
    pltpu.make_async_copy(dst.at[most], dst.at[most], recv_sem).wait()
    own.wait()


def share_start(y, src, dst, columns, send_sem, recv_sem, own_sem):
    up, down = (y + 1) % 4, (y + 3) % 4
    own = pltpu.make_async_copy(
        src.at[:, :, :, columns], dst.at[:, y, :, :, columns], own_sem
    )
    own.start()

    def send(block, slot, c, target, lane):
        copy = pltpu.make_async_remote_copy(
            src_ref=block,
            dst_ref=dst.at[:, slot, c, :, columns],
            send_sem=send_sem.at[lane, c],
            recv_sem=recv_sem.at[lane, c],
            device_id={"y": target},
            device_id_type=BY_MESH,
        )
        copy.start()
        return copy

    ups, downs = {}, {}
    for step in range(4):
        c, d = step, (step + 2) % 4
        ups[c] = send(src.at[:, c, :, columns], y, c, up, 0)
        downs[d] = send(src.at[:, d, :, columns], y, d, down, 1)

    far = []

    def forward():
        for step in range(2):
            c, d = step, step + 2
            ups[c].wait_recv()
            far.append(send(dst.at[:, down, c, :, columns], down, c, up, 2))
            downs[d].wait_recv()
            far.append(send(dst.at[:, up, d, :, columns], up, d, down, 2))

    def finish():
        for step in range(2):
            ups[step + 2].wait_recv()
            downs[step].wait_recv()
        for copy in far:
            copy.wait_recv()
        for copy in (*ups.values(), *downs.values(), *far):
            copy.wait_send()
        own.wait()

    return forward, finish


def pack(arrays, into, columns):
    row = lax.broadcasted_iota(jnp.int32, (64, 64), 0)
    column = lax.broadcasted_iota(jnp.int32, (64, 64), 1)
    wanted = ((row // 4) % 4) * 16 + (row // 16) * 4 + row % 4
    order = jnp.where(column == wanted, 1.0, 0.0).astype(BF16)

    def body(group, carry):
        rows = pl.ds(pl.multiple_of(group * 16, 16), 16)
        block = jnp.concatenate([arrays[at, rows, columns] for at in range(4)], axis=0)
        ordered = jnp.dot(order, block, preferred_element_type=F32).astype(BF16)
        into[pl.ds(group * 4, 4)] = ordered.reshape(4, 16, WIDTH)
        return carry

    lax.fori_loop(0, 16, body, 0)


def attend(moved, heads, grads, chunk):
    heads[...] = pltpu.einshape("abk->bak", moved[...].astype(F32)).astype(BF16)
    scale = 1.0 / HD**0.5
    row = lax.broadcasted_iota(jnp.int32, (128, 128), 0)
    column = lax.broadcasted_iota(jnp.int32, (128, 128), 1)
    same = row // 64 == column // 64

    def dot(a, b, over_a, over_b):
        return lax.dot_general(
            a, b, (((over_a,), (over_b,)), ((), ())), preferred_element_type=F32
        )

    def body(pair, carry):
        patches = pl.ds(pair * 2, 2)
        for head in range(WIDTH // HD):
            lanes = slice(head * HD, (head + 1) * HD)
            q, k, v, g = (
                heads[pl.ds(array * 4 + pair * 2, 2), :, lanes].reshape(128, HD)
                for array in range(4)
            )
            scores = jnp.where(same, dot(q, k, 1, 1) * scale, -1e30)
            weight = jnp.exp(scores - jnp.max(scores, axis=1, keepdims=True))
            probs = weight / jnp.sum(weight, axis=1, keepdims=True)
            probs_b = probs.astype(BF16)
            attended = dot(probs_b, v, 1, 0)
            delta = jnp.sum(g.astype(F32) * attended, axis=1, keepdims=True)
            grad_scores = (probs * (dot(g, v, 1, 1) - delta)).astype(BF16)
            results = (
                dot(grad_scores, k, 1, 0) * scale,
                dot(grad_scores, q, 0, 0) * scale,
                dot(probs_b, g, 0, 0),
            )
            out = pl.ds(chunk * WIDTH + head * HD, HD)
            for m, result in enumerate(results):
                grads[m, patches, :, out] = result.astype(BF16).reshape(2, 64, HD)
        return carry

    lax.fori_loop(0, 2, body, 0)


def rows_start(place, own_rows, rows, send_sem, recv_sem, own_sem):
    z, y, x = place
    steps = (0, 3, 2, 1)

    def block(b, at_x, part=slice(None)):
        return rows.at[:, ((z + steps[b]) % 4) * 4 + at_x, part]

    def send(src, dst, axis, target, lane, b):
        copy = pltpu.make_async_remote_copy(
            src_ref=src,
            dst_ref=dst,
            send_sem=send_sem.at[lane, b],
            recv_sem=recv_sem.at[lane, b],
            device_id={axis: target},
            device_id_type=BY_MESH,
        )
        copy.start()
        return copy

    z_up, z_down, x_up, x_down = (z + 1) % 4, (z + 3) % 4, (x + 1) % 4, (x + 3) % 4
    own = pltpu.make_async_copy(own_rows, block(0, x), own_sem)
    own.start()
    z_ups = send(own_rows, block(0, x), "z", z_up, 0, 0)
    z_downs = send(own_rows, block(0, x), "z", z_down, 0, 1)
    z_far, ups, downs, far = [], {}, {}, {}

    def along_x(b):
        src = own_rows if b == 0 else block(b, x)
        ups[b] = send(src, block(b, x), "x", x_up, 1, b)
        downs[b] = send(src, block(b, x), "x", x_down, 2, b)

    along_x(0)

    def near():
        low, high = pl.ds(0, 32), pl.ds(32, 32)
        z_ups.wait_recv()
        z_far.append(send(block(1, x, low), block(1, x, low), "z", z_up, 0, 2))
        along_x(1)
        z_downs.wait_recv()
        z_far.append(send(block(3, x, high), block(3, x, high), "z", z_down, 0, 3))
        along_x(3)

    def across():
        for copy in z_far:
            copy.wait_recv()
        along_x(2)

    def forward(b):
        if b < 2:
            ups[b].wait_recv()
            far[b] = send(block(b, x_down), block(b, x_down), "x", x_up, 3, b)
        else:
            downs[b].wait_recv()
            far[b] = send(block(b, x_up), block(b, x_up), "x", x_down, 3, b)

    def finish():
        for b in range(4):
            (downs if b < 2 else ups)[b].wait_recv()
            far[b].wait_recv()
        for copy in (z_ups, z_downs, *z_far, *ups.values(), *downs.values(), *far.values()):
            copy.wait_send()
        own.wait()

    return near, across, forward, finish


def front_kernel(
    query, key_in, value, grad_out, own_rows, shared, rows, local, packed, moved, heads, grads, *sems
):
    place = position()
    sems = list(sems)
    loads = [
        pltpu.make_async_copy(ref, local.at[at], sems[0].at[at])
        for at, ref in enumerate((query, key_in, value, grad_out))
    ]
    for load in loads:
        load.start()
    rows_sems = sems[1:4]
    swap_sems = [sems[4 + 3 * chunk : 7 + 3 * chunk] for chunk in range(CHUNKS)]
    share_sems = [sems[4 + 3 * chunk : 7 + 3 * chunk] for chunk in range(CHUNKS, 2 * CHUNKS)]
    greet_all(place)
    for load in loads:
        load.wait()
    swaps = []

    def swap_out(chunk):
        pack(local, packed.at[chunk], pl.ds(chunk * WIDTH, WIDTH))
        swaps.append(swap_start(place, packed.at[chunk], moved.at[chunk], *swap_sems[chunk]))

    swap_out(0)
    near, across, pass_on, rows_finish = rows_start(place, own_rows, rows, *rows_sems)
    for chunk in range(1, CHUNKS):
        swap_out(chunk)
    forwards, finishes = [], []

    def swapped(chunk):
        swap_wait(swaps[chunk], packed.at[chunk], moved.at[chunk], *swap_sems[chunk][:2])
        attend(moved.at[chunk], heads, grads, chunk)
        columns = pl.ds(chunk * WIDTH, WIDTH)
        forward, finish = share_start(place[1], grads, shared, columns, *share_sems[chunk])
        forwards.append(forward)
        finishes.append(finish)

    swapped(0)
    near()
    pass_on(0)
    forwards[0]()
    swapped(1)
    across()
    forwards[1]()
    pass_on(1)
    swapped(2)
    pass_on(3)
    forwards[2]()
    swapped(3)
    pass_on(2)
    forwards[3]()
    for finish in finishes:
        finish()
    rows_finish()


SWAP_SEMS = [pltpu.SemaphoreType.DMA] * 3
SHARE_SEMS = [
    pltpu.SemaphoreType.DMA((3, 4)),
    pltpu.SemaphoreType.DMA((3, 4)),
    pltpu.SemaphoreType.DMA,
]
ROWS_SEMS = [
    pltpu.SemaphoreType.DMA((4, 4)),
    pltpu.SemaphoreType.DMA((4, 4)),
    pltpu.SemaphoreType.DMA,
]
VMEM = pl.BlockSpec(memory_space=pltpu.VMEM)


def params(collective_id):
    return pltpu.CompilerParams(
        collective_id=collective_id, has_side_effects=True, vmem_limit_bytes=32 << 20
    )


def front(*arrays):
    return pl.pallas_call(
        front_kernel,
        out_shape=(
            jax.ShapeDtypeStruct((3, 4, 4, 64, 1024), BF16),
            jax.ShapeDtypeStruct((3, 16, 64, 1024), BF16),
        ),
        in_specs=[pl.BlockSpec(memory_space=pltpu.HBM)] * 5,
        out_specs=(ANY, ANY),
        scratch_shapes=[
            pltpu.VMEM((4, 256, 1024), BF16),
            pltpu.VMEM((CHUNKS, 64, 16, WIDTH), BF16),
            pltpu.VMEM((CHUNKS, 64, 16, WIDTH), BF16),
            pltpu.VMEM((16, 64, WIDTH), BF16),
            pltpu.VMEM((3, 4, 64, 1024), BF16),
            pltpu.SemaphoreType.DMA((4,)),
            *ROWS_SEMS,
            *SWAP_SEMS * CHUNKS,
            *SHARE_SEMS * CHUNKS,
        ],
        compiler_params=params(1),
        name="front",
    )(*arrays)


def deliver_kernel(part, dst, other, total, core_send, core_recv, send_sem, recv_sem, own_sem):
    z, y, x = position()
    zl, core = lax.axis_index("zl"), lax.axis_index("c")
    slot = ((y * 4 + z) * 4 + x) * 2 + zl
    barrier = pltpu.get_barrier_semaphore()

    def peer(step):
        return tm_peer((z, y, x), step)

    def greet(first, half):
        def body(step, carry):
            pl.semaphore_signal(
                barrier, inc=1, device_id={**peer(step), "zl": half}, device_id_type=BY_MESH
            )
            return carry

        lax.fori_loop(first, 64, body, 0)

    pl.semaphore_signal(barrier, inc=1, device_id={"c": 1 - core}, device_id_type=BY_MESH)
    greet(0, 1 - zl)
    greet(1, zl)
    pl.semaphore_wait(barrier, 128)

    halves = (1 - zl, zl)
    copies = []
    for at, half in enumerate(halves):
        copy = pltpu.make_async_remote_copy(
            src_ref=part.at[2 * half + 1 - core],
            dst_ref=other.at[at],
            send_sem=core_send.at[at],
            recv_sem=core_recv.at[at],
            device_id={"c": 1 - core},
            device_id_type=BY_MESH,
        )
        copy.start()
        copies.append(copy)
    for at, half in enumerate(halves):
        copies[at].wait_recv()
        both = part[2 * half + core].astype(F32) + other[at].astype(F32)
        total[at] = pltpu.einshape("abk->bak", both.reshape(16, 64, 256)).astype(BF16)

        def send(step, carry):
            to = peer(step)
            pltpu.make_async_remote_copy(
                src_ref=total.at[at, tm_index(to)],
                dst_ref=dst.at[slot],
                send_sem=send_sem,
                recv_sem=recv_sem,
                device_id={**to, "zl": half},
                device_id_type=BY_MESH,
            ).start()
            return carry

        lax.fori_loop(at, 64, send, 0)
    own = pltpu.make_async_copy(total.at[1, z * 16 + y * 4 + x], dst.at[slot], own_sem)
    own.start()
    most = dst.at[pl.ds(0, 127)]
    pltpu.make_async_copy(most, most, send_sem).wait()
    pltpu.make_async_copy(most, most, recv_sem).wait()
    for copy in copies:
        copy.wait_send()
    own.wait()


def deliver(part):
    return pl.pallas_call(
        deliver_kernel,
        out_shape=jax.ShapeDtypeStruct((128, 16, 256), part.dtype),
        in_specs=[pl.BlockSpec(memory_space=pltpu.VMEM)],
        out_specs=ANY,
        scratch_shapes=[
            pltpu.VMEM((2, 1024, 256), part.dtype),
            pltpu.VMEM((2, 64, 16, 256), part.dtype),
            pltpu.SemaphoreType.DMA((2,)),
            pltpu.SemaphoreType.DMA((2,)),
            pltpu.SemaphoreType.DMA,
            pltpu.SemaphoreType.DMA,
            pltpu.SemaphoreType.DMA,
        ],
        compiler_params=params(2),
        name="deliver",
    )(part)


def patch_order():
    z, x, _, slot, c = np.indices((4, 4, 2, 4, 4)).reshape(5, 512)
    return np.eye(256, dtype=np.float32)[4 * (z * 16 + slot * 4 + x) + c]


def per_device(query, key_in, value, grad_out, weights):
    shared, rows = front(query, key_in, value, grad_out, weights)
    partial_sum = jnp.einsum(
        "mtk,mzik->zti",
        shared.reshape(3, 1024, 1024),
        rows.reshape(3, 4, 256, 1024),
        preferred_element_type=F32,
    )
    back = deliver(partial_sum.astype(BF16)).reshape(4, 512, 256)
    place = jnp.asarray(patch_order(), BF16)
    out = jnp.einsum("ytk,tp->ykp", back, place, preferred_element_type=F32)
    return out.reshape(1024, 256).astype(BF16)


def solution(mesh):
    fine = Mesh(mesh.devices.reshape(4, 4, 4, 2, 2), AXES)
    placed = (P(TM, HEAD),) * 4 + (P(None, TM, HEAD),)
    return jax.shard_map(
        per_device, mesh=fine, in_specs=placed, out_specs=P(HEAD, TM), check_vma=False
    )
```

```python
import jax
import jax.numpy as jnp
import numpy as np
from jax import lax
from jax.experimental import pallas as pl
from jax.experimental.pallas import tpu as pltpu
from jax.sharding import Mesh, PartitionSpec as P

HD = 128
CHUNKS = 4
WIDTH = 1024 // CHUNKS
AXES = ("z", "y", "x", "zl", "c")
TM = AXES[:3]
HEAD = AXES[3:]
BF16 = jnp.bfloat16
F32 = jnp.float32
BY_MESH = pl.DeviceIdType.MESH
ANY = pl.BlockSpec(memory_space=pl.ANY)


def position():
    return lax.axis_index("z"), lax.axis_index("y"), lax.axis_index("x")


def tm_peer(place, step):
    z, y, x = place
    return {
        "z": (z + step // 16) % 4,
        "y": (y + (step // 4) % 4) % 4,
        "x": (x + step % 4) % 4,
    }


def tm_index(at):
    return at["z"] * 16 + at["y"] * 4 + at["x"]


def greet_all(place, zl, core):
    barrier = pltpu.get_barrier_semaphore()

    def greet(half):
        def body(step, carry):
            to = {**tm_peer(place, step), "zl": half}
            pl.semaphore_signal(barrier, inc=1, device_id=to, device_id_type=BY_MESH)
            return carry

        return body

    pl.semaphore_signal(barrier, inc=1, device_id={"c": 1 - core}, device_id_type=BY_MESH)
    lax.fori_loop(1, 64, greet(zl), 0)
    lax.fori_loop(0, 64, greet(1 - zl), 0)
    pl.semaphore_wait(barrier, 128)


def swap_start(place, src, dst, send_sem, recv_sem, own_sem):
    me = tm_index(tm_peer(place, 0))
    own = pltpu.make_async_copy(src.at[me], dst.at[me], own_sem)
    own.start()

    def send(step, carry):
        to = tm_peer(place, step)
        pltpu.make_async_remote_copy(
            src_ref=src.at[tm_index(to)],
            dst_ref=dst.at[me],
            send_sem=send_sem,
            recv_sem=recv_sem,
            device_id=to,
            device_id_type=BY_MESH,
        ).start()
        return carry

    lax.fori_loop(1, 64, send, 0)
    return own


def swap_wait(own, src, dst, send_sem, recv_sem):
    most = pl.ds(0, 63)
    pltpu.make_async_copy(src.at[most], src.at[most], send_sem).wait()
    pltpu.make_async_copy(dst.at[most], dst.at[most], recv_sem).wait()
    own.wait()


def share_start(y, src, dst, columns, send_sem, recv_sem, own_sem):
    up, down = (y + 1) % 4, (y + 3) % 4
    own = pltpu.make_async_copy(
        src.at[:, :, :, columns], dst.at[:, y, :, :, columns], own_sem
    )
    own.start()

    def send(block, slot, c, target, lane):
        copy = pltpu.make_async_remote_copy(
            src_ref=block,
            dst_ref=dst.at[:, slot, c, :, columns],
            send_sem=send_sem.at[lane, c],
            recv_sem=recv_sem.at[lane, c],
            device_id={"y": target},
            device_id_type=BY_MESH,
        )
        copy.start()
        return copy

    ups, downs = {}, {}
    for step in range(4):
        c, d = step, (step + 2) % 4
        ups[c] = send(src.at[:, c, :, columns], y, c, up, 0)
        downs[d] = send(src.at[:, d, :, columns], y, d, down, 1)

    far = []

    def forward():
        for step in range(2):
            c, d = step, step + 2
            ups[c].wait_recv()
            far.append(send(dst.at[:, down, c, :, columns], down, c, up, 2))
            downs[d].wait_recv()
            far.append(send(dst.at[:, up, d, :, columns], up, d, down, 2))

    def finish():
        for step in range(2):
            ups[step + 2].wait_recv()
            downs[step].wait_recv()
        for copy in far:
            copy.wait_recv()
        for copy in (*ups.values(), *downs.values(), *far):
            copy.wait_send()
        own.wait()

    return forward, finish


def pack(arrays, into, columns):
    row = lax.broadcasted_iota(jnp.int32, (64, 64), 0)
    column = lax.broadcasted_iota(jnp.int32, (64, 64), 1)
    wanted = ((row // 4) % 4) * 16 + (row // 16) * 4 + row % 4
    order = jnp.where(column == wanted, 1.0, 0.0).astype(BF16)

    def body(group, carry):
        rows = pl.ds(pl.multiple_of(group * 16, 16), 16)
        block = jnp.concatenate([arrays[at, rows, columns] for at in range(4)], axis=0)
        ordered = jnp.dot(order, block, preferred_element_type=F32).astype(BF16)
        into[pl.ds(group * 4, 4)] = ordered.reshape(4, 16, WIDTH)
        return carry

    lax.fori_loop(0, 16, body, 0)


def attend(moved, heads, grads, chunk):
    heads[...] = pltpu.einshape("abk->bak", moved[...].astype(F32)).astype(BF16)
    scale = 1.0 / HD**0.5
    row = lax.broadcasted_iota(jnp.int32, (128, 128), 0)
    column = lax.broadcasted_iota(jnp.int32, (128, 128), 1)
    same = row // 64 == column // 64

    def dot(a, b, over_a, over_b):
        return lax.dot_general(
            a, b, (((over_a,), (over_b,)), ((), ())), preferred_element_type=F32
        )

    def body(pair, carry):
        patches = pl.ds(pair * 2, 2)
        for head in range(WIDTH // HD):
            lanes = slice(head * HD, (head + 1) * HD)
            q, k, v, g = (
                heads[pl.ds(array * 4 + pair * 2, 2), :, lanes].reshape(128, HD)
                for array in range(4)
            )
            scores = jnp.where(same, dot(q, k, 1, 1) * scale, -1e30)
            weight = jnp.exp(scores - jnp.max(scores, axis=1, keepdims=True))
            probs = weight / jnp.sum(weight, axis=1, keepdims=True)
            probs_b = probs.astype(BF16)
            attended = dot(probs_b, v, 1, 0)
            delta = jnp.sum(g.astype(F32) * attended, axis=1, keepdims=True)
            grad_scores = (probs * (dot(g, v, 1, 1) - delta)).astype(BF16)
            results = (
                dot(grad_scores, k, 1, 0) * scale,
                dot(grad_scores, q, 0, 0) * scale,
                dot(probs_b, g, 0, 0),
            )
            out = pl.ds(chunk * WIDTH + head * HD, HD)
            for m, result in enumerate(results):
                grads[m, patches, :, out] = result.astype(BF16).reshape(2, 64, HD)
        return carry

    lax.fori_loop(0, 2, body, 0)


def rows_start(place, own_rows, rows, send_sem, recv_sem, own_sem):
    z, y, x = place
    steps = (0, 3, 2, 1)

    def block(b, at_x, part=slice(None)):
        return rows.at[:, ((z + steps[b]) % 4) * 4 + at_x, part]

    def send(src, dst, axis, target, lane, b):
        copy = pltpu.make_async_remote_copy(
            src_ref=src,
            dst_ref=dst,
            send_sem=send_sem.at[lane, b],
            recv_sem=recv_sem.at[lane, b],
            device_id={axis: target},
            device_id_type=BY_MESH,
        )
        copy.start()
        return copy

    z_up, z_down, x_up, x_down = (z + 1) % 4, (z + 3) % 4, (x + 1) % 4, (x + 3) % 4
    own = pltpu.make_async_copy(own_rows, block(0, x), own_sem)
    own.start()
    z_ups = send(own_rows, block(0, x), "z", z_up, 0, 0)
    z_downs = send(own_rows, block(0, x), "z", z_down, 0, 1)
    z_far, ups, downs, far = [], {}, {}, {}

    def along_x(b):
        src = own_rows if b == 0 else block(b, x)
        ups[b] = send(src, block(b, x), "x", x_up, 1, b)
        downs[b] = send(src, block(b, x), "x", x_down, 2, b)

    along_x(0)

    def near():
        low, high = pl.ds(0, 32), pl.ds(32, 32)
        z_ups.wait_recv()
        z_far.append(send(block(1, x, low), block(1, x, low), "z", z_up, 0, 2))
        along_x(1)
        z_downs.wait_recv()
        z_far.append(send(block(3, x, high), block(3, x, high), "z", z_down, 0, 3))
        along_x(3)

    def across():
        for copy in z_far:
            copy.wait_recv()
        along_x(2)

    def forward(b):
        if b < 2:
            ups[b].wait_recv()
            far[b] = send(block(b, x_down), block(b, x_down), "x", x_up, 3, b)
        else:
            downs[b].wait_recv()
            far[b] = send(block(b, x_up), block(b, x_up), "x", x_down, 3, b)

    def finish():
        for b in range(4):
            (downs if b < 2 else ups)[b].wait_recv()
            far[b].wait_recv()
        for copy in (z_ups, z_downs, *z_far, *ups.values(), *downs.values(), *far.values()):
            copy.wait_send()
        own.wait()

    return near, across, forward, finish


def multiply(shared, rows, hg, slot, first_chunk, chunks):
    columns = pl.ds(first_chunk * WIDTH, chunks * WIDTH)
    product = None
    for m in range(3):
        term = lax.dot_general(
            shared[m, slot, :, :, columns].reshape(256, chunks * WIDTH),
            rows[m, pl.ds(hg * 4, 4), :, columns].reshape(256, chunks * WIDTH),
            (((1,), (1,)), ((), ())),
            preferred_element_type=F32,
        )
        product = term if product is None else product + term
    return product


def whole_kernel(
    query, key_in, value, grad_out, own_rows, dst, shared, rows, local, packed, moved, heads, grads,
    part, leaving, other, total, *sems
):
    place = position()
    z, y, x = place
    zl, core = lax.axis_index("zl"), lax.axis_index("c")
    sems = list(sems)
    loads = [
        pltpu.make_async_copy(ref, local.at[at], sems[0].at[at])
        for at, ref in enumerate((query, key_in, value, grad_out))
    ]
    for load in loads:
        load.start()
    rows_sems = sems[1:4]
    core_send, core_recv, send_sem, recv_sem, own_sem = sems[4:9]
    swap_sems = [sems[9 + 3 * chunk : 12 + 3 * chunk] for chunk in range(CHUNKS)]
    share_sems = [sems[9 + 3 * chunk : 12 + 3 * chunk] for chunk in range(CHUNKS, 2 * CHUNKS)]
    greet_all(place, zl, core)
    for load in loads:
        load.wait()
    swaps = []

    def swap_out(chunk):
        pack(local, packed.at[chunk], pl.ds(chunk * WIDTH, WIDTH))
        swaps.append(swap_start(place, packed.at[chunk], moved.at[chunk], *swap_sems[chunk]))

    swap_out(0)
    near, across, pass_on, rows_finish = rows_start(place, own_rows, rows, *rows_sems)
    for chunk in range(1, CHUNKS):
        swap_out(chunk)
    forwards, finishes = [], []

    def swapped(chunk):
        swap_wait(swaps[chunk], packed.at[chunk], moved.at[chunk], *swap_sems[chunk][:2])
        attend(moved.at[chunk], heads, grads, chunk)
        columns = pl.ds(chunk * WIDTH, WIDTH)
        forward, finish = share_start(y, grads, shared, columns, *share_sems[chunk])
        forwards.append(forward)
        finishes.append(finish)

    swapped(0)
    near()
    pass_on(0)
    forwards[0]()
    swapped(1)
    across()
    forwards[1]()
    pass_on(1)
    swapped(2)
    pass_on(3)
    forwards[2]()
    swapped(3)
    pass_on(2)
    forwards[3]()
    for finish in finishes[:3]:
        finish()
    rows_finish()

    def most(at, carry):
        hg, slot = at // 4, at % 4
        part[hg, pl.ds(slot * 256, 256)] = multiply(shared, rows, hg, slot, 0, 3)
        return carry

    lax.fori_loop(0, 16, most, 0)
    finishes[3]()

    halves = (1 - zl, zl)
    copies = []
    for at, half in enumerate(halves):
        theirs = 2 * half + 1 - core

        def last(slot, carry):
            tokens = pl.ds(pl.multiple_of(slot * 256, 256), 256)
            product = part[theirs, tokens] + multiply(shared, rows, theirs, slot, 3, 1)
            leaving[at, tokens] = product.astype(BF16)
            return carry

        lax.fori_loop(0, 4, last, 0)
        copy = pltpu.make_async_remote_copy(
            src_ref=leaving.at[at],
            dst_ref=other.at[at],
            send_sem=core_send.at[at],
            recv_sem=core_recv.at[at],
            device_id={"c": 1 - core},
            device_id_type=BY_MESH,
        )
        copy.start()
        copies.append(copy)
    slot_here = ((y * 4 + z) * 4 + x) * 2 + zl
    for at, half in enumerate(halves):
        mine = 2 * half + core

        def last(slot, carry):
            tokens = pl.ds(pl.multiple_of(slot * 256, 256), 256)
            part[mine, tokens] += multiply(shared, rows, mine, slot, 3, 1)
            return carry

        lax.fori_loop(0, 4, last, 0)
        copies[at].wait_recv()
        both = part[mine] + other[at].astype(F32)
        total[at] = pltpu.einshape("abk->bak", both.reshape(16, 64, 256)).astype(BF16)

        def send(step, carry):
            to = tm_peer(place, step)
            pltpu.make_async_remote_copy(
                src_ref=total.at[at, tm_index(to)],
                dst_ref=dst.at[slot_here],
                send_sem=send_sem,
                recv_sem=recv_sem,
                device_id={**to, "zl": half},
                device_id_type=BY_MESH,
            ).start()
            return carry

        lax.fori_loop(at, 64, send, 0)
    own = pltpu.make_async_copy(
        total.at[1, tm_index(tm_peer(place, 0))], dst.at[slot_here], own_sem
    )
    own.start()
    rest = dst.at[pl.ds(0, 127)]
    pltpu.make_async_copy(rest, rest, send_sem).wait()
    pltpu.make_async_copy(rest, rest, recv_sem).wait()
    for copy in copies:
        copy.wait_send()
    own.wait()


SWAP_SEMS = [pltpu.SemaphoreType.DMA] * 3
SHARE_SEMS = [
    pltpu.SemaphoreType.DMA((3, 4)),
    pltpu.SemaphoreType.DMA((3, 4)),
    pltpu.SemaphoreType.DMA,
]
ROWS_SEMS = [
    pltpu.SemaphoreType.DMA((4, 4)),
    pltpu.SemaphoreType.DMA((4, 4)),
    pltpu.SemaphoreType.DMA,
]
CORE_SEMS = [pltpu.SemaphoreType.DMA((2,)), pltpu.SemaphoreType.DMA((2,))]


def whole(*arrays):
    return pl.pallas_call(
        whole_kernel,
        out_shape=jax.ShapeDtypeStruct((128, 16, 256), BF16),
        in_specs=[pl.BlockSpec(memory_space=pltpu.HBM)] * 5,
        out_specs=ANY,
        scratch_shapes=[
            pltpu.VMEM((3, 4, 4, 64, 1024), BF16),
            pltpu.VMEM((3, 16, 64, 1024), BF16),
            pltpu.VMEM((4, 256, 1024), BF16),
            pltpu.VMEM((CHUNKS, 64, 16, WIDTH), BF16),
            pltpu.VMEM((CHUNKS, 64, 16, WIDTH), BF16),
            pltpu.VMEM((16, 64, WIDTH), BF16),
            pltpu.VMEM((3, 4, 64, 1024), BF16),
            pltpu.VMEM((4, 1024, 256), F32),
            pltpu.VMEM((2, 1024, 256), BF16),
            pltpu.VMEM((2, 1024, 256), BF16),
            pltpu.VMEM((2, 64, 16, 256), BF16),
            pltpu.SemaphoreType.DMA((4,)),
            *ROWS_SEMS,
            *CORE_SEMS,
            *SWAP_SEMS,
            *SWAP_SEMS * CHUNKS,
            *SHARE_SEMS * CHUNKS,
        ],
        compiler_params=pltpu.CompilerParams(
            collective_id=1, has_side_effects=True, vmem_limit_bytes=56 << 20
        ),
        name="whole",
    )(*(pltpu.with_memory_space_constraint(array, pltpu.HBM) for array in arrays))


def patch_order():
    z, x, _, slot, c = np.indices((4, 4, 2, 4, 4)).reshape(5, 512)
    return np.eye(256, dtype=np.float32)[4 * (z * 16 + slot * 4 + x) + c]


def per_device(query, key_in, value, grad_out, weights):
    back = whole(query, key_in, value, grad_out, weights).reshape(4, 512, 256)
    place = jnp.asarray(patch_order(), BF16)
    out = jnp.einsum("ytk,tp->ykp", back, place, preferred_element_type=F32)
    return out.reshape(1024, 256).astype(BF16)


def solution(mesh):
    fine = Mesh(mesh.devices.reshape(4, 4, 4, 2, 2), AXES)
    placed = (P(TM, HEAD),) * 4 + (P(None, TM, HEAD),)
    return jax.shard_map(
        per_device, mesh=fine, in_specs=placed, out_specs=P(HEAD, TM), check_vma=False
    )
```

```python
import jax
import jax.numpy as jnp
import numpy as np
from jax import lax
from jax.experimental import pallas as pl
from jax.experimental.pallas import tpu as pltpu
from jax.sharding import Mesh, PartitionSpec as P

HD = 128
CHUNKS = 4
WIDTH = 1024 // CHUNKS
AXES = ("z", "y", "x", "zl", "c")
TM = AXES[:3]
HEAD = AXES[3:]
BF16 = jnp.bfloat16
F32 = jnp.float32
BY_MESH = pl.DeviceIdType.MESH
ANY = pl.BlockSpec(memory_space=pl.ANY)


def position():
    return lax.axis_index("z"), lax.axis_index("y"), lax.axis_index("x")


def tm_peer(place, step):
    z, y, x = place
    return {
        "z": (z + step // 16) % 4,
        "y": (y + (step // 4) % 4) % 4,
        "x": (x + step % 4) % 4,
    }


def tm_index(at):
    return at["z"] * 16 + at["y"] * 4 + at["x"]


def greet_all(place, zl, core):
    barrier = pltpu.get_barrier_semaphore()

    def greet(half):
        def body(step, carry):
            to = {**tm_peer(place, step), "zl": half}
            pl.semaphore_signal(barrier, inc=1, device_id=to, device_id_type=BY_MESH)
            return carry

        return body

    pl.semaphore_signal(barrier, inc=1, device_id={"c": 1 - core}, device_id_type=BY_MESH)
    lax.fori_loop(1, 64, greet(zl), 0)
    lax.fori_loop(0, 64, greet(1 - zl), 0)
    pl.semaphore_wait(barrier, 128)


def swap_start(place, src, dst, send_sem, recv_sem, own_sem):
    me = tm_index(tm_peer(place, 0))
    own = pltpu.make_async_copy(src.at[me], dst.at[me], own_sem)
    own.start()

    def send(step, carry):
        to = tm_peer(place, step)
        pltpu.make_async_remote_copy(
            src_ref=src.at[tm_index(to)],
            dst_ref=dst.at[me],
            send_sem=send_sem,
            recv_sem=recv_sem,
            device_id=to,
            device_id_type=BY_MESH,
        ).start()
        return carry

    lax.fori_loop(1, 64, send, 0)
    return own


def swap_wait(own, src, dst, send_sem, recv_sem):
    most = pl.ds(0, 63)
    pltpu.make_async_copy(src.at[most], src.at[most], send_sem).wait()
    pltpu.make_async_copy(dst.at[most], dst.at[most], recv_sem).wait()
    own.wait()


def share_start(y, src, dst, columns, send_sem, recv_sem, own_sem):
    up, down = (y + 1) % 4, (y + 3) % 4
    own = pltpu.make_async_copy(
        src.at[:, :, :, columns], dst.at[:, y, :, :, columns], own_sem
    )
    own.start()

    def send(block, slot, c, target, lane):
        copy = pltpu.make_async_remote_copy(
            src_ref=block,
            dst_ref=dst.at[:, slot, c, :, columns],
            send_sem=send_sem.at[lane, c],
            recv_sem=recv_sem.at[lane, c],
            device_id={"y": target},
            device_id_type=BY_MESH,
        )
        copy.start()
        return copy

    ups, downs = {}, {}
    for step in range(4):
        c, d = step, (step + 2) % 4
        ups[c] = send(src.at[:, c, :, columns], y, c, up, 0)
        downs[d] = send(src.at[:, d, :, columns], y, d, down, 1)

    far = []

    def forward():
        for step in range(2):
            c, d = step, step + 2
            ups[c].wait_recv()
            far.append(send(dst.at[:, down, c, :, columns], down, c, up, 2))
            downs[d].wait_recv()
            far.append(send(dst.at[:, up, d, :, columns], up, d, down, 2))

    def finish():
        for step in range(2):
            ups[step + 2].wait_recv()
            downs[step].wait_recv()
        for copy in far:
            copy.wait_recv()
        for copy in (*ups.values(), *downs.values(), *far):
            copy.wait_send()
        own.wait()

    return forward, finish


def pack(arrays, into, columns):
    row = lax.broadcasted_iota(jnp.int32, (64, 64), 0)
    column = lax.broadcasted_iota(jnp.int32, (64, 64), 1)
    wanted = ((row // 4) % 4) * 16 + (row // 16) * 4 + row % 4
    order = jnp.where(column == wanted, 1.0, 0.0).astype(BF16)

    def body(group, carry):
        rows = pl.ds(pl.multiple_of(group * 16, 16), 16)
        block = jnp.concatenate([arrays[at, rows, columns] for at in range(4)], axis=0)
        ordered = jnp.dot(order, block, preferred_element_type=F32).astype(BF16)
        into[pl.ds(group * 4, 4)] = ordered.reshape(4, 16, WIDTH)
        return carry

    lax.fori_loop(0, 16, body, 0)


def attend(moved, heads, grads, chunk):
    heads[...] = pltpu.einshape("abk->bak", moved[...].astype(F32)).astype(BF16)
    scale = 1.0 / HD**0.5
    row = lax.broadcasted_iota(jnp.int32, (128, 128), 0)
    column = lax.broadcasted_iota(jnp.int32, (128, 128), 1)
    same = row // 64 == column // 64

    def dot(a, b, over_a, over_b):
        return lax.dot_general(
            a, b, (((over_a,), (over_b,)), ((), ())), preferred_element_type=F32
        )

    def body(pair, carry):
        patches = pl.ds(pair * 2, 2)
        for head in range(WIDTH // HD):
            lanes = slice(head * HD, (head + 1) * HD)
            q, k, v, g = (
                heads[pl.ds(array * 4 + pair * 2, 2), :, lanes].reshape(128, HD)
                for array in range(4)
            )
            scores = jnp.where(same, dot(q, k, 1, 1) * scale, -1e30)
            weight = jnp.exp(scores - jnp.max(scores, axis=1, keepdims=True))
            probs = weight / jnp.sum(weight, axis=1, keepdims=True)
            probs_b = probs.astype(BF16)
            attended = dot(probs_b, v, 1, 0)
            delta = jnp.sum(g.astype(F32) * attended, axis=1, keepdims=True)
            grad_scores = (probs * (dot(g, v, 1, 1) - delta)).astype(BF16)
            results = (
                dot(grad_scores, k, 1, 0) * scale,
                dot(grad_scores, q, 0, 0) * scale,
                dot(probs_b, g, 0, 0),
            )
            out = pl.ds(chunk * WIDTH + head * HD, HD)
            for m, result in enumerate(results):
                grads[m, patches, :, out] = result.astype(BF16).reshape(2, 64, HD)
        return carry

    lax.fori_loop(0, 2, body, 0)


def rows_start(place, own_rows, rows, send_sem, recv_sem, own_sem):
    z, y, x = place
    steps = (0, 3, 2, 1)

    def block(b, at_x, part=slice(None)):
        return rows.at[:, ((z + steps[b]) % 4) * 4 + at_x, part]

    def send(src, dst, axis, target, lane, b):
        copy = pltpu.make_async_remote_copy(
            src_ref=src,
            dst_ref=dst,
            send_sem=send_sem.at[lane, b],
            recv_sem=recv_sem.at[lane, b],
            device_id={axis: target},
            device_id_type=BY_MESH,
        )
        copy.start()
        return copy

    z_up, z_down, x_up, x_down = (z + 1) % 4, (z + 3) % 4, (x + 1) % 4, (x + 3) % 4
    own = pltpu.make_async_copy(own_rows, block(0, x), own_sem)
    own.start()
    z_ups = send(own_rows, block(0, x), "z", z_up, 0, 0)
    z_downs = send(own_rows, block(0, x), "z", z_down, 0, 1)
    z_far, ups, downs, far = [], {}, {}, {}

    def along_x(b):
        src = own_rows if b == 0 else block(b, x)
        ups[b] = send(src, block(b, x), "x", x_up, 1, b)
        downs[b] = send(src, block(b, x), "x", x_down, 2, b)

    along_x(0)

    def near():
        low, high = pl.ds(0, 32), pl.ds(32, 32)
        z_ups.wait_recv()
        z_far.append(send(block(1, x, low), block(1, x, low), "z", z_up, 0, 2))
        along_x(1)
        z_downs.wait_recv()
        z_far.append(send(block(3, x, high), block(3, x, high), "z", z_down, 0, 3))
        along_x(3)

    def across():
        for copy in z_far:
            copy.wait_recv()
        along_x(2)

    def forward(b):
        if b < 2:
            ups[b].wait_recv()
            far[b] = send(block(b, x_down), block(b, x_down), "x", x_up, 3, b)
        else:
            downs[b].wait_recv()
            far[b] = send(block(b, x_up), block(b, x_up), "x", x_down, 3, b)

    def finish():
        for b in range(4):
            (downs if b < 2 else ups)[b].wait_recv()
            far[b].wait_recv()
        for copy in (z_ups, z_downs, *z_far, *ups.values(), *downs.values(), *far.values()):
            copy.wait_send()
        own.wait()

    return near, across, forward, finish


def multiply(shared, rows, hg, slot, first_chunk, chunks):
    columns = pl.ds(first_chunk * WIDTH, chunks * WIDTH)
    product = None
    for m in range(3):
        term = lax.dot_general(
            shared[m, slot, :, :, columns].reshape(256, chunks * WIDTH),
            rows[m, pl.ds(hg * 4, 4), :, columns].reshape(256, chunks * WIDTH),
            (((1,), (1,)), ((), ())),
            preferred_element_type=F32,
        )
        product = term if product is None else product + term
    return product


def whole_kernel(
    query, key_in, value, grad_out, own_rows, dst, shared, rows, local, packed, moved, heads, grads,
    part, leaving, other, total, *sems
):
    place = position()
    z, y, x = place
    zl, core = lax.axis_index("zl"), lax.axis_index("c")
    sems = list(sems)
    loads = [
        pltpu.make_async_copy(ref, local.at[at], sems[0].at[at])
        for at, ref in enumerate((query, key_in, value, grad_out))
    ]
    for load in loads:
        load.start()
    rows_sems = sems[1:4]
    core_send, core_recv, send_sem, recv_sem, own_sem = sems[4:9]
    swap_sems = [sems[9 + 3 * chunk : 12 + 3 * chunk] for chunk in range(CHUNKS)]
    share_sems = [sems[9 + 3 * chunk : 12 + 3 * chunk] for chunk in range(CHUNKS, 2 * CHUNKS)]
    greet_all(place, zl, core)
    swaps = []

    def pack_up(chunk):
        pack(local, packed.at[chunk], pl.ds(chunk * WIDTH, WIDTH))

    def swap_out(chunk):
        swaps.append(swap_start(place, packed.at[chunk], moved.at[chunk], *swap_sems[chunk]))

    forwards, finishes = [], []

    def swapped(chunk, following=None):
        swap_wait(swaps[chunk], packed.at[chunk], moved.at[chunk], *swap_sems[chunk][:2])
        if following is not None:
            swap_out(following)
        attend(moved.at[chunk], heads, grads, chunk)
        columns = pl.ds(chunk * WIDTH, WIDTH)
        forward, finish = share_start(y, grads, shared, columns, *share_sems[chunk])
        forwards.append(forward)
        finishes.append(finish)

    near, across, pass_on, rows_finish = rows_start(place, own_rows, rows, *rows_sems)
    for load in loads:
        load.wait()
    pack_up(0)
    swap_out(0)
    for chunk in range(1, CHUNKS):
        pack_up(chunk)
    near()
    swap_out(1)
    swapped(0, following=2)
    pass_on(0)
    across()
    swapped(1, following=3)
    forwards[0]()
    pass_on(1)
    swapped(2)
    forwards[1]()
    pass_on(3)
    swapped(3)
    forwards[2]()
    pass_on(2)
    forwards[3]()
    for finish in finishes[:3]:
        finish()
    rows_finish()

    def most(at, carry):
        hg, slot = at // 4, at % 4
        part[hg, pl.ds(slot * 256, 256)] = multiply(shared, rows, hg, slot, 0, 3)
        return carry

    lax.fori_loop(0, 16, most, 0)
    finishes[3]()

    halves = (1 - zl, zl)
    copies = []
    for at, half in enumerate(halves):
        theirs = 2 * half + 1 - core

        def last(slot, carry):
            tokens = pl.ds(pl.multiple_of(slot * 256, 256), 256)
            product = part[theirs, tokens] + multiply(shared, rows, theirs, slot, 3, 1)
            leaving[at, tokens] = product.astype(BF16)
            return carry

        lax.fori_loop(0, 4, last, 0)
        copy = pltpu.make_async_remote_copy(
            src_ref=leaving.at[at],
            dst_ref=other.at[at],
            send_sem=core_send.at[at],
            recv_sem=core_recv.at[at],
            device_id={"c": 1 - core},
            device_id_type=BY_MESH,
        )
        copy.start()
        copies.append(copy)
    slot_here = ((y * 4 + z) * 4 + x) * 2 + zl
    for at, half in enumerate(halves):
        mine = 2 * half + core

        def last(slot, carry):
            tokens = pl.ds(pl.multiple_of(slot * 256, 256), 256)
            part[mine, tokens] += multiply(shared, rows, mine, slot, 3, 1)
            return carry

        lax.fori_loop(0, 4, last, 0)
        copies[at].wait_recv()
        both = part[mine] + other[at].astype(F32)
        total[at] = pltpu.einshape("abk->bak", both.reshape(16, 64, 256)).astype(BF16)

        def send(step, carry):
            to = tm_peer(place, step)
            pltpu.make_async_remote_copy(
                src_ref=total.at[at, tm_index(to)],
                dst_ref=dst.at[slot_here],
                send_sem=send_sem,
                recv_sem=recv_sem,
                device_id={**to, "zl": half},
                device_id_type=BY_MESH,
            ).start()
            return carry

        lax.fori_loop(at, 64, send, 0)
    own = pltpu.make_async_copy(
        total.at[1, tm_index(tm_peer(place, 0))], dst.at[slot_here], own_sem
    )
    own.start()
    rest = dst.at[pl.ds(0, 127)]
    pltpu.make_async_copy(rest, rest, send_sem).wait()
    pltpu.make_async_copy(rest, rest, recv_sem).wait()
    for copy in copies:
        copy.wait_send()
    own.wait()


SWAP_SEMS = [pltpu.SemaphoreType.DMA] * 3
SHARE_SEMS = [
    pltpu.SemaphoreType.DMA((3, 4)),
    pltpu.SemaphoreType.DMA((3, 4)),
    pltpu.SemaphoreType.DMA,
]
ROWS_SEMS = [
    pltpu.SemaphoreType.DMA((4, 4)),
    pltpu.SemaphoreType.DMA((4, 4)),
    pltpu.SemaphoreType.DMA,
]
CORE_SEMS = [pltpu.SemaphoreType.DMA((2,)), pltpu.SemaphoreType.DMA((2,))]


def whole(*arrays):
    return pl.pallas_call(
        whole_kernel,
        out_shape=jax.ShapeDtypeStruct((128, 16, 256), BF16),
        in_specs=[pl.BlockSpec(memory_space=pltpu.HBM)] * 5,
        out_specs=ANY,
        scratch_shapes=[
            pltpu.VMEM((3, 4, 4, 64, 1024), BF16),
            pltpu.VMEM((3, 16, 64, 1024), BF16),
            pltpu.VMEM((4, 256, 1024), BF16),
            pltpu.VMEM((CHUNKS, 64, 16, WIDTH), BF16),
            pltpu.VMEM((CHUNKS, 64, 16, WIDTH), BF16),
            pltpu.VMEM((16, 64, WIDTH), BF16),
            pltpu.VMEM((3, 4, 64, 1024), BF16),
            pltpu.VMEM((4, 1024, 256), F32),
            pltpu.VMEM((2, 1024, 256), BF16),
            pltpu.VMEM((2, 1024, 256), BF16),
            pltpu.VMEM((2, 64, 16, 256), BF16),
            pltpu.SemaphoreType.DMA((4,)),
            *ROWS_SEMS,
            *CORE_SEMS,
            *SWAP_SEMS,
            *SWAP_SEMS * CHUNKS,
            *SHARE_SEMS * CHUNKS,
        ],
        compiler_params=pltpu.CompilerParams(
            collective_id=1, has_side_effects=True, vmem_limit_bytes=56 << 20
        ),
        name="whole",
    )(*(pltpu.with_memory_space_constraint(array, pltpu.HBM) for array in arrays))


def patch_order():
    z, x, _, slot, c = np.indices((4, 4, 2, 4, 4)).reshape(5, 512)
    return np.eye(256, dtype=np.float32)[4 * (z * 16 + slot * 4 + x) + c]


def per_device(query, key_in, value, grad_out, weights):
    back = whole(query, key_in, value, grad_out, weights).reshape(4, 512, 256)
    place = jnp.asarray(patch_order(), BF16)
    out = jnp.einsum("ytk,tp->ykp", back, place, preferred_element_type=F32)
    return out.reshape(1024, 256).astype(BF16)


def solution(mesh):
    fine = Mesh(mesh.devices.reshape(4, 4, 4, 2, 2), AXES)
    placed = (P(TM, HEAD),) * 4 + (P(None, TM, HEAD),)
    return jax.shard_map(
        per_device, mesh=fine, in_specs=placed, out_specs=P(HEAD, TM), check_vma=False
    )
```

```python
import functools

import jax
import jax.numpy as jnp
import numpy as np
from jax import lax
from jax.experimental import pallas as pl
from jax.experimental.pallas import tpu as pltpu
from jax.sharding import Mesh, PartitionSpec as P

HD = 128
CHUNKS = 4
WIDTH = 1024 // CHUNKS
AXES = ("z", "y", "x", "zl", "c")
TM = AXES[:3]
HEAD = AXES[3:]
BF16 = jnp.bfloat16
F32 = jnp.float32
BY_MESH = pl.DeviceIdType.MESH
ANY = pl.BlockSpec(memory_space=pl.ANY)


def position():
    return lax.axis_index("z"), lax.axis_index("y"), lax.axis_index("x")


def tm_peer(place, step):
    z, y, x = place
    return {
        "z": (z + step // 16) % 4,
        "y": (y + (step // 4) % 4) % 4,
        "x": (x + step % 4) % 4,
    }


def tm_index(at):
    return at["z"] * 16 + at["y"] * 4 + at["x"]


def greet_all(place, zl, core):
    barrier = pltpu.get_barrier_semaphore()

    def greet(half):
        def body(step, carry):
            to = {**tm_peer(place, step), "zl": half}
            pl.semaphore_signal(barrier, inc=1, device_id=to, device_id_type=BY_MESH)
            return carry

        return body

    pl.semaphore_signal(barrier, inc=1, device_id={"c": 1 - core}, device_id_type=BY_MESH)
    lax.fori_loop(1, 64, greet(zl), 0)
    lax.fori_loop(0, 64, greet(1 - zl), 0)
    pl.semaphore_wait(barrier, 128)


def swap_own(place, src, dst, send_sem, recv_sem, own_sem):
    me = tm_index(tm_peer(place, 0))
    own = pltpu.make_async_copy(src.at[me], dst.at[me], own_sem)
    own.start()
    return own


def swap_start(place, src, dst, send_sem, recv_sem, own_sem):
    me = tm_index(tm_peer(place, 0))

    def send(step, carry):
        to = tm_peer(place, step)
        pltpu.make_async_remote_copy(
            src_ref=src.at[tm_index(to)],
            dst_ref=dst.at[me],
            send_sem=send_sem,
            recv_sem=recv_sem,
            device_id=to,
            device_id_type=BY_MESH,
        ).start()
        return carry

    lax.fori_loop(1, 64, send, 0)


def swap_wait(own, src, dst, send_sem, recv_sem):
    most = pl.ds(0, 63)
    pltpu.make_async_copy(src.at[most], src.at[most], send_sem).wait()
    pltpu.make_async_copy(dst.at[most], dst.at[most], recv_sem).wait()
    own.wait()


def share_start(y, src, dst, columns, send_sem, recv_sem, own_sem):
    up, down = (y + 1) % 4, (y + 3) % 4
    own = pltpu.make_async_copy(
        src.at[:, :, :, columns], dst.at[:, y, :, :, columns], own_sem
    )
    own.start()

    def send(block, slot, c, target, lane):
        copy = pltpu.make_async_remote_copy(
            src_ref=block,
            dst_ref=dst.at[:, slot, c, :, columns],
            send_sem=send_sem.at[lane, c],
            recv_sem=recv_sem.at[lane, c],
            device_id={"y": target},
            device_id_type=BY_MESH,
        )
        copy.start()
        return copy

    ups, downs = {}, {}
    for step in range(4):
        c, d = step, (step + 2) % 4
        ups[c] = send(src.at[:, c, :, columns], y, c, up, 0)
        downs[d] = send(src.at[:, d, :, columns], y, d, down, 1)

    far = []

    def forward():
        for step in range(2):
            c, d = step, step + 2
            ups[c].wait_recv()
            far.append(send(dst.at[:, down, c, :, columns], down, c, up, 2))
            downs[d].wait_recv()
            far.append(send(dst.at[:, up, d, :, columns], up, d, down, 2))

    def finish():
        for step in range(2):
            ups[step + 2].wait_recv()
            downs[step].wait_recv()
        for copy in far:
            copy.wait_recv()
        for copy in (*ups.values(), *downs.values(), *far):
            copy.wait_send()
        own.wait()

    return forward, finish


def pack(arrays, into, columns):
    row = lax.broadcasted_iota(jnp.int32, (64, 64), 0)
    column = lax.broadcasted_iota(jnp.int32, (64, 64), 1)
    wanted = ((row // 4) % 4) * 16 + (row // 16) * 4 + row % 4
    order = jnp.where(column == wanted, 1.0, 0.0).astype(BF16)

    def body(group, carry):
        rows = pl.ds(pl.multiple_of(group * 16, 16), 16)
        block = jnp.concatenate([arrays[at, rows, columns] for at in range(4)], axis=0)
        ordered = jnp.dot(order, block, preferred_element_type=F32).astype(BF16)
        into[pl.ds(group * 4, 4)] = ordered.reshape(4, 16, WIDTH)
        return carry

    lax.fori_loop(0, 16, body, 0)


def attend(moved, heads, grads, chunk):
    heads[...] = pltpu.einshape("abk->bak", moved[...].astype(F32)).astype(BF16)
    scale = 1.0 / HD**0.5
    row = lax.broadcasted_iota(jnp.int32, (128, 128), 0)
    column = lax.broadcasted_iota(jnp.int32, (128, 128), 1)
    same = row // 64 == column // 64

    def dot(a, b, over_a, over_b):
        return lax.dot_general(
            a, b, (((over_a,), (over_b,)), ((), ())), preferred_element_type=F32
        )

    def body(pair, carry):
        patches = pl.ds(pair * 2, 2)
        for head in range(WIDTH // HD):
            lanes = slice(head * HD, (head + 1) * HD)
            q, k, v, g = (
                heads[pl.ds(array * 4 + pair * 2, 2), :, lanes].reshape(128, HD)
                for array in range(4)
            )
            scores = jnp.where(same, dot(q, k, 1, 1) * scale, -1e30)
            weight = jnp.exp(scores - jnp.max(scores, axis=1, keepdims=True))
            probs = weight / jnp.sum(weight, axis=1, keepdims=True)
            probs_b = probs.astype(BF16)
            attended = dot(probs_b, v, 1, 0)
            delta = jnp.sum(g.astype(F32) * attended, axis=1, keepdims=True)
            grad_scores = (probs * (dot(g, v, 1, 1) - delta)).astype(BF16)
            results = (
                dot(grad_scores, k, 1, 0) * scale,
                dot(grad_scores, q, 0, 0) * scale,
                dot(probs_b, g, 0, 0),
            )
            out = pl.ds(chunk * WIDTH + head * HD, HD)
            for m, result in enumerate(results):
                grads[m, patches, :, out] = result.astype(BF16).reshape(2, 64, HD)
        return carry

    lax.fori_loop(0, 2, body, 0)


def rows_start(place, own_rows, rows, send_sem, recv_sem, own_sem):
    z, y, x = place
    steps = (0, 3, 2, 1)

    def block(b, at_x, part=slice(None)):
        return rows.at[:, ((z + steps[b]) % 4) * 4 + at_x, part]

    def plan(src, dst, axis, target, lane, b):
        return pltpu.make_async_remote_copy(
            src_ref=src,
            dst_ref=dst,
            send_sem=send_sem.at[lane, b],
            recv_sem=recv_sem.at[lane, b],
            device_id={axis: target},
            device_id_type=BY_MESH,
        )

    z_up, z_down, x_up, x_down = (z + 1) % 4, (z + 3) % 4, (x + 1) % 4, (x + 3) % 4
    low, high = pl.ds(0, 32), pl.ds(32, 32)
    z_ups = plan(own_rows, block(0, x), "z", z_up, 0, 0)
    z_downs = plan(own_rows, block(0, x), "z", z_down, 0, 1)
    z_far = (
        plan(block(1, x, low), block(1, x, low), "z", z_up, 0, 2),
        plan(block(3, x, high), block(3, x, high), "z", z_down, 0, 3),
    )
    ups, downs, far = [], [], []
    for b in range(4):
        src = own_rows if b == 0 else block(b, x)
        ups.append(plan(src, block(b, x), "x", x_up, 1, b))
        downs.append(plan(src, block(b, x), "x", x_down, 2, b))
        at, target = (x_down, x_up) if b < 2 else (x_up, x_down)
        far.append(plan(block(b, at), block(b, at), "x", target, 3, b))
    own = pltpu.make_async_copy(own_rows, block(0, x), own_sem)
    own.start()
    ups[0].start()
    downs[0].start()

    def along_z():
        z_ups.start()
        z_downs.start()

    def near():
        for copy, onward, b in ((z_ups, z_far[0], 1), (z_downs, z_far[1], 3)):
            copy.wait_recv()
            onward.start()
            ups[b].start()
            downs[b].start()

    def across():
        for copy in z_far:
            copy.wait_recv()
        ups[2].start()
        downs[2].start()

    def forward(b):
        (ups if b < 2 else downs)[b].wait_recv()
        far[b].start()

    def finish():
        for b in range(4):
            (downs if b < 2 else ups)[b].wait_recv()
            far[b].wait_recv()
        for copy in (z_ups, z_downs, *z_far, *ups, *downs, *far):
            copy.wait_send()
        own.wait()

    return along_z, near, across, forward, finish


def multiply(shared, rows, hg, slot, first_chunk, chunks):
    columns = pl.ds(first_chunk * WIDTH, chunks * WIDTH)
    product = None
    for m in range(3):
        term = lax.dot_general(
            shared[m, slot, :, :, columns].reshape(256, chunks * WIDTH),
            rows[m, pl.ds(hg * 4, 4), :, columns].reshape(256, chunks * WIDTH),
            (((1,), (1,)), ((), ())),
            preferred_element_type=F32,
        )
        product = term if product is None else product + term
    return product


def whole_kernel(
    query, key_in, value, grad_out, own_rows, dst, shared, rows, local, packed, moved, heads, grads,
    part, leaving, other, total, *sems
):
    place = position()
    z, y, x = place
    zl, core = lax.axis_index("zl"), lax.axis_index("c")
    sems = list(sems)
    loads = [
        pltpu.make_async_copy(ref, local.at[at], sems[0].at[at])
        for at, ref in enumerate((query, key_in, value, grad_out))
    ]
    for load in loads:
        load.start()
    rows_sems = sems[1:4]
    core_send, core_recv, send_sem, recv_sem, own_sem = sems[4:9]
    swap_sems = [sems[9 + 3 * chunk : 12 + 3 * chunk] for chunk in range(CHUNKS)]
    share_sems = [sems[9 + 3 * chunk : 12 + 3 * chunk] for chunk in range(CHUNKS, 2 * CHUNKS)]
    greet_all(place, zl, core)
    swaps, forwards, finishes = [], [], []

    def swap_out(chunk):
        swap_start(place, packed.at[chunk], moved.at[chunk], *swap_sems[chunk])

    def swapped(chunk):
        swap_wait(swaps[chunk], packed.at[chunk], moved.at[chunk], *swap_sems[chunk][:2])
        attend(moved.at[chunk], heads, grads, chunk)
        columns = pl.ds(chunk * WIDTH, WIDTH)
        forward, finish = share_start(y, grads, shared, columns, *share_sems[chunk])
        forwards.append(forward)
        finishes.append(finish)

    swaps_first, rows_first = pl.when(zl == 0), pl.when(zl == 1)
    along_z, near, across, pass_on, rows_finish = rows_start(place, own_rows, rows, *rows_sems)
    rows_first(along_z)
    for load in loads:
        load.wait()
    for chunk in range(CHUNKS):
        pack(local, packed.at[chunk], pl.ds(chunk * WIDTH, WIDTH))
        swaps.append(swap_own(place, packed.at[chunk], moved.at[chunk], *swap_sems[chunk]))
        swaps_first(functools.partial(swap_out, chunk))

    @rows_first
    def _():
        near()
        for chunk in range(CHUNKS):
            swap_out(chunk)

    swapped(0)
    pass_on(0)
    swapped(1)
    swaps_first(along_z)
    forwards[0]()
    rows_first(across)
    swapped(2)
    forwards[1]()
    swaps_first(near)

    @rows_first
    def _():
        pass_on(1)
        pass_on(3)

    swapped(3)
    forwards[2]()

    @swaps_first
    def _():
        across()
        pass_on(1)
        pass_on(3)

    pass_on(2)
    forwards[3]()
    for finish in finishes[:3]:
        finish()
    rows_finish()

    def most(at, carry):
        hg, slot = at // 4, at % 4
        part[hg, pl.ds(slot * 256, 256)] = multiply(shared, rows, hg, slot, 0, 3)
        return carry

    lax.fori_loop(0, 16, most, 0)
    finishes[3]()

    halves = (1 - zl, zl)
    copies = []
    for at, half in enumerate(halves):
        theirs = 2 * half + 1 - core

        def last(slot, carry):
            tokens = pl.ds(pl.multiple_of(slot * 256, 256), 256)
            product = part[theirs, tokens] + multiply(shared, rows, theirs, slot, 3, 1)
            leaving[at, tokens] = product.astype(BF16)
            return carry

        lax.fori_loop(0, 4, last, 0)
        copy = pltpu.make_async_remote_copy(
            src_ref=leaving.at[at],
            dst_ref=other.at[at],
            send_sem=core_send.at[at],
            recv_sem=core_recv.at[at],
            device_id={"c": 1 - core},
            device_id_type=BY_MESH,
        )
        copy.start()
        copies.append(copy)
    slot_here = ((y * 4 + z) * 4 + x) * 2 + zl
    for at, half in enumerate(halves):
        mine = 2 * half + core

        def last(slot, carry):
            tokens = pl.ds(pl.multiple_of(slot * 256, 256), 256)
            part[mine, tokens] += multiply(shared, rows, mine, slot, 3, 1)
            return carry

        lax.fori_loop(0, 4, last, 0)
        copies[at].wait_recv()
        both = part[mine] + other[at].astype(F32)
        total[at] = pltpu.einshape("abk->bak", both.reshape(16, 64, 256)).astype(BF16)

        def send(step, carry):
            to = tm_peer(place, step)
            pltpu.make_async_remote_copy(
                src_ref=total.at[at, tm_index(to)],
                dst_ref=dst.at[slot_here],
                send_sem=send_sem,
                recv_sem=recv_sem,
                device_id={**to, "zl": half},
                device_id_type=BY_MESH,
            ).start()
            return carry

        lax.fori_loop(at, 64, send, 0)
    own = pltpu.make_async_copy(
        total.at[1, tm_index(tm_peer(place, 0))], dst.at[slot_here], own_sem
    )
    own.start()
    rest = dst.at[pl.ds(0, 127)]
    pltpu.make_async_copy(rest, rest, send_sem).wait()
    pltpu.make_async_copy(rest, rest, recv_sem).wait()
    for copy in copies:
        copy.wait_send()
    own.wait()


SWAP_SEMS = [pltpu.SemaphoreType.DMA] * 3
SHARE_SEMS = [
    pltpu.SemaphoreType.DMA((3, 4)),
    pltpu.SemaphoreType.DMA((3, 4)),
    pltpu.SemaphoreType.DMA,
]
ROWS_SEMS = [
    pltpu.SemaphoreType.DMA((4, 4)),
    pltpu.SemaphoreType.DMA((4, 4)),
    pltpu.SemaphoreType.DMA,
]
CORE_SEMS = [pltpu.SemaphoreType.DMA((2,)), pltpu.SemaphoreType.DMA((2,))]


def whole(*arrays):
    return pl.pallas_call(
        whole_kernel,
        out_shape=jax.ShapeDtypeStruct((128, 16, 256), BF16),
        in_specs=[pl.BlockSpec(memory_space=pltpu.HBM)] * 5,
        out_specs=ANY,
        scratch_shapes=[
            pltpu.VMEM((3, 4, 4, 64, 1024), BF16),
            pltpu.VMEM((3, 16, 64, 1024), BF16),
            pltpu.VMEM((4, 256, 1024), BF16),
            pltpu.VMEM((CHUNKS, 64, 16, WIDTH), BF16),
            pltpu.VMEM((CHUNKS, 64, 16, WIDTH), BF16),
            pltpu.VMEM((16, 64, WIDTH), BF16),
            pltpu.VMEM((3, 4, 64, 1024), BF16),
            pltpu.VMEM((4, 1024, 256), F32),
            pltpu.VMEM((2, 1024, 256), BF16),
            pltpu.VMEM((2, 1024, 256), BF16),
            pltpu.VMEM((2, 64, 16, 256), BF16),
            pltpu.SemaphoreType.DMA((4,)),
            *ROWS_SEMS,
            *CORE_SEMS,
            *SWAP_SEMS,
            *SWAP_SEMS * CHUNKS,
            *SHARE_SEMS * CHUNKS,
        ],
        compiler_params=pltpu.CompilerParams(
            collective_id=1, has_side_effects=True, vmem_limit_bytes=56 << 20
        ),
        name="whole",
    )(*(pltpu.with_memory_space_constraint(array, pltpu.HBM) for array in arrays))


def patch_order():
    z, x, _, slot, c = np.indices((4, 4, 2, 4, 4)).reshape(5, 512)
    return np.eye(256, dtype=np.float32)[4 * (z * 16 + slot * 4 + x) + c]


def per_device(query, key_in, value, grad_out, weights):
    back = whole(query, key_in, value, grad_out, weights).reshape(4, 512, 256)
    place = jnp.asarray(patch_order(), BF16)
    out = jnp.einsum("ytk,tp->ykp", back, place, preferred_element_type=F32)
    return out.reshape(1024, 256).astype(BF16)


def solution(mesh):
    fine = Mesh(mesh.devices.reshape(4, 4, 4, 2, 2), AXES)
    placed = (P(TM, HEAD),) * 4 + (P(None, TM, HEAD),)
    return jax.shard_map(
        per_device, mesh=fine, in_specs=placed, out_specs=P(HEAD, TM), check_vma=False
    )
```

```python
import functools

import jax
import jax.numpy as jnp
import numpy as np
from jax import lax
from jax.experimental import pallas as pl
from jax.experimental.pallas import tpu as pltpu
from jax.sharding import Mesh, PartitionSpec as P

HD = 128
CHUNKS = 4
WIDTH = 1024 // CHUNKS
AXES = ("z", "y", "x", "zl", "c")
TM = AXES[:3]
HEAD = AXES[3:]
BF16 = jnp.bfloat16
F32 = jnp.float32
BY_MESH = pl.DeviceIdType.MESH
ANY = pl.BlockSpec(memory_space=pl.ANY)


def position():
    return lax.axis_index("z"), lax.axis_index("y"), lax.axis_index("x")


def turn(at, by):
    return lax.rem(at + by, jnp.int32(4))


def tm_peer(place, step):
    z, y, x = place
    step = jnp.int32(step)
    by_x, rest = lax.rem(step, jnp.int32(4)), lax.div(step, jnp.int32(4))
    by_y, by_z = lax.rem(rest, jnp.int32(4)), lax.div(rest, jnp.int32(4))
    return {"z": turn(z, by_z), "y": turn(y, by_y), "x": turn(x, by_x)}


def tm_index(at):
    return at["z"] * 16 + at["y"] * 4 + at["x"]


def greet_all(place, zl, core):
    barrier = pltpu.get_barrier_semaphore()

    def greet(half):
        def body(step, carry):
            to = {**tm_peer(place, step), "zl": half}
            pl.semaphore_signal(barrier, inc=1, device_id=to, device_id_type=BY_MESH)
            return carry

        return body

    pl.semaphore_signal(barrier, inc=1, device_id={"c": 1 - core}, device_id_type=BY_MESH)
    lax.fori_loop(1, 64, greet(zl), 0, unroll=7)
    lax.fori_loop(0, 64, greet(1 - zl), 0, unroll=8)
    pl.semaphore_wait(barrier, 128)


def swap_own(place, src, dst, send_sem, recv_sem, own_sem):
    me = tm_index(tm_peer(place, 0))
    own = pltpu.make_async_copy(src.at[me], dst.at[me], own_sem)
    own.start()
    return own


def swap_start(place, src, dst, send_sem, recv_sem, own_sem):
    me = tm_index(tm_peer(place, 0))

    def send(step, carry):
        to = tm_peer(place, step)
        pltpu.make_async_remote_copy(
            src_ref=src.at[tm_index(to)],
            dst_ref=dst.at[me],
            send_sem=send_sem,
            recv_sem=recv_sem,
            device_id=to,
            device_id_type=BY_MESH,
        ).start()
        return carry

    lax.fori_loop(1, 64, send, 0, unroll=7)


def swap_wait(own, src, dst, send_sem, recv_sem):
    most = pl.ds(0, 63)
    pltpu.make_async_copy(src.at[most], src.at[most], send_sem).wait()
    pltpu.make_async_copy(dst.at[most], dst.at[most], recv_sem).wait()
    own.wait()


def share_start(y, src, dst, columns, send_sem, recv_sem, own_sem):
    up, down = (y + 1) % 4, (y + 3) % 4
    own = pltpu.make_async_copy(
        src.at[:, :, :, columns], dst.at[:, y, :, :, columns], own_sem
    )
    own.start()

    def send(block, slot, c, target, lane):
        copy = pltpu.make_async_remote_copy(
            src_ref=block,
            dst_ref=dst.at[:, slot, c, :, columns],
            send_sem=send_sem.at[lane, c],
            recv_sem=recv_sem.at[lane, c],
            device_id={"y": target},
            device_id_type=BY_MESH,
        )
        copy.start()
        return copy

    ups, downs = {}, {}
    for step in range(4):
        c, d = step, (step + 2) % 4
        ups[c] = send(src.at[:, c, :, columns], y, c, up, 0)
        downs[d] = send(src.at[:, d, :, columns], y, d, down, 1)

    far = []

    def forward():
        for step in range(2):
            c, d = step, step + 2
            ups[c].wait_recv()
            far.append(send(dst.at[:, down, c, :, columns], down, c, up, 2))
            downs[d].wait_recv()
            far.append(send(dst.at[:, up, d, :, columns], up, d, down, 2))

    def finish():
        for step in range(2):
            ups[step + 2].wait_recv()
            downs[step].wait_recv()
        for copy in far:
            copy.wait_recv()
        for copy in (*ups.values(), *downs.values(), *far):
            copy.wait_send()
        own.wait()

    return forward, finish


def pack(arrays, into, columns):
    row = lax.broadcasted_iota(jnp.int32, (64, 64), 0)
    column = lax.broadcasted_iota(jnp.int32, (64, 64), 1)
    wanted = ((row // 4) % 4) * 16 + (row // 16) * 4 + row % 4
    order = jnp.where(column == wanted, 1.0, 0.0).astype(BF16)

    def body(group, carry):
        rows = pl.ds(pl.multiple_of(group * 16, 16), 16)
        block = jnp.concatenate([arrays[at, rows, columns] for at in range(4)], axis=0)
        ordered = jnp.dot(order, block, preferred_element_type=F32).astype(BF16)
        into[pl.ds(group * 4, 4)] = ordered.reshape(4, 16, WIDTH)
        return carry

    lax.fori_loop(0, 16, body, 0)


def attend(moved, heads, grads, chunk):
    heads[...] = pltpu.einshape("abk->bak", moved[...].astype(F32)).astype(BF16)
    scale = 1.0 / HD**0.5
    row = lax.broadcasted_iota(jnp.int32, (128, 128), 0)
    column = lax.broadcasted_iota(jnp.int32, (128, 128), 1)
    same = row // 64 == column // 64

    def dot(a, b, over_a, over_b):
        return lax.dot_general(
            a, b, (((over_a,), (over_b,)), ((), ())), preferred_element_type=F32
        )

    def body(pair, carry):
        patches = pl.ds(pair * 2, 2)
        for head in range(WIDTH // HD):
            lanes = slice(head * HD, (head + 1) * HD)
            q, k, v, g = (
                heads[pl.ds(array * 4 + pair * 2, 2), :, lanes].reshape(128, HD)
                for array in range(4)
            )
            scores = jnp.where(same, dot(q, k, 1, 1) * scale, -1e30)
            weight = jnp.exp(scores - jnp.max(scores, axis=1, keepdims=True))
            probs = weight / jnp.sum(weight, axis=1, keepdims=True)
            probs_b = probs.astype(BF16)
            attended = dot(probs_b, v, 1, 0)
            delta = jnp.sum(g.astype(F32) * attended, axis=1, keepdims=True)
            grad_scores = (probs * (dot(g, v, 1, 1) - delta)).astype(BF16)
            results = (
                dot(grad_scores, k, 1, 0) * scale,
                dot(grad_scores, q, 0, 0) * scale,
                dot(probs_b, g, 0, 0),
            )
            out = pl.ds(chunk * WIDTH + head * HD, HD)
            for m, result in enumerate(results):
                grads[m, patches, :, out] = result.astype(BF16).reshape(2, 64, HD)
        return carry

    lax.fori_loop(0, 2, body, 0)


def rows_start(place, own_rows, rows, send_sem, recv_sem, own_sem):
    z, y, x = place
    steps = (0, 3, 2, 1)

    def block(b, at_x, part=slice(None)):
        return rows.at[:, ((z + steps[b]) % 4) * 4 + at_x, part]

    def plan(src, dst, axis, target, lane, b):
        return pltpu.make_async_remote_copy(
            src_ref=src,
            dst_ref=dst,
            send_sem=send_sem.at[lane, b],
            recv_sem=recv_sem.at[lane, b],
            device_id={axis: target},
            device_id_type=BY_MESH,
        )

    z_up, z_down, x_up, x_down = (z + 1) % 4, (z + 3) % 4, (x + 1) % 4, (x + 3) % 4
    low, high = pl.ds(0, 32), pl.ds(32, 32)
    z_ups = plan(own_rows, block(0, x), "z", z_up, 0, 0)
    z_downs = plan(own_rows, block(0, x), "z", z_down, 0, 1)
    z_far = (
        plan(block(1, x, low), block(1, x, low), "z", z_up, 0, 2),
        plan(block(3, x, high), block(3, x, high), "z", z_down, 0, 3),
    )
    ups, downs, far = [], [], []
    for b in range(4):
        src = own_rows if b == 0 else block(b, x)
        ups.append(plan(src, block(b, x), "x", x_up, 1, b))
        downs.append(plan(src, block(b, x), "x", x_down, 2, b))
        at, target = (x_down, x_up) if b < 2 else (x_up, x_down)
        far.append(plan(block(b, at), block(b, at), "x", target, 3, b))
    own = pltpu.make_async_copy(own_rows, block(0, x), own_sem)
    own.start()
    ups[0].start()
    downs[0].start()

    def along_z():
        z_ups.start()
        z_downs.start()

    def near():
        for copy, onward, b in ((z_ups, z_far[0], 1), (z_downs, z_far[1], 3)):
            copy.wait_recv()
            onward.start()
            ups[b].start()
            downs[b].start()

    def across():
        for copy in z_far:
            copy.wait_recv()
        ups[2].start()
        downs[2].start()

    def forward(b):
        (ups if b < 2 else downs)[b].wait_recv()
        far[b].start()

    def finish():
        for b in range(4):
            (downs if b < 2 else ups)[b].wait_recv()
            far[b].wait_recv()
        for copy in (z_ups, z_downs, *z_far, *ups, *downs, *far):
            copy.wait_send()
        own.wait()

    return along_z, near, across, forward, finish


def multiply(shared, rows, hg, slot, first_chunk, chunks):
    columns = pl.ds(first_chunk * WIDTH, chunks * WIDTH)
    product = None
    for m in range(3):
        term = lax.dot_general(
            shared[m, slot, :, :, columns].reshape(256, chunks * WIDTH),
            rows[m, pl.ds(hg * 4, 4), :, columns].reshape(256, chunks * WIDTH),
            (((1,), (1,)), ((), ())),
            preferred_element_type=F32,
        )
        product = term if product is None else product + term
    return product


def whole_kernel(
    query, key_in, value, grad_out, own_rows, dst, shared, rows, local, packed, moved, heads, grads,
    part, leaving, other, total, *sems
):
    place = position()
    z, y, x = place
    zl, core = lax.axis_index("zl"), lax.axis_index("c")
    sems = list(sems)
    loads = [
        pltpu.make_async_copy(ref, local.at[at], sems[0].at[at])
        for at, ref in enumerate((query, key_in, value, grad_out))
    ]
    for load in loads:
        load.start()
    rows_sems = sems[1:4]
    core_send, core_recv, send_sem, recv_sem, own_sem = sems[4:9]
    swap_sems = [sems[9 + 3 * chunk : 12 + 3 * chunk] for chunk in range(CHUNKS)]
    share_sems = [sems[9 + 3 * chunk : 12 + 3 * chunk] for chunk in range(CHUNKS, 2 * CHUNKS)]
    greet_all(place, zl, core)
    swaps, forwards, finishes = [], [], []

    def swap_out(chunk):
        swap_start(place, packed.at[chunk], moved.at[chunk], *swap_sems[chunk])

    def swapped(chunk):
        swap_wait(swaps[chunk], packed.at[chunk], moved.at[chunk], *swap_sems[chunk][:2])
        attend(moved.at[chunk], heads, grads, chunk)
        columns = pl.ds(chunk * WIDTH, WIDTH)
        forward, finish = share_start(y, grads, shared, columns, *share_sems[chunk])
        forwards.append(forward)
        finishes.append(finish)

    swaps_first, rows_first = pl.when(zl == 0), pl.when(zl == 1)
    along_z, near, across, pass_on, rows_finish = rows_start(place, own_rows, rows, *rows_sems)
    rows_first(along_z)
    for load in loads:
        load.wait()
    for chunk in range(CHUNKS):
        pack(local, packed.at[chunk], pl.ds(chunk * WIDTH, WIDTH))
        swaps.append(swap_own(place, packed.at[chunk], moved.at[chunk], *swap_sems[chunk]))
        swaps_first(functools.partial(swap_out, chunk))

    @rows_first
    def _():
        near()
        for chunk in range(CHUNKS):
            swap_out(chunk)

    swapped(0)
    pass_on(0)
    swapped(1)
    swaps_first(along_z)
    forwards[0]()
    rows_first(across)
    swapped(2)
    forwards[1]()
    swaps_first(near)

    @rows_first
    def _():
        pass_on(1)
        pass_on(3)

    swapped(3)
    forwards[2]()

    @swaps_first
    def _():
        across()
        pass_on(1)
        pass_on(3)

    pass_on(2)
    forwards[3]()
    for finish in finishes[:3]:
        finish()
    rows_finish()

    def most(at, carry):
        hg, slot = at // 4, at % 4
        part[hg, pl.ds(slot * 256, 256)] = multiply(shared, rows, hg, slot, 0, 3)
        return carry

    lax.fori_loop(0, 16, most, 0)
    finishes[3]()

    halves = (1 - zl, zl)
    copies = []
    for at, half in enumerate(halves):
        theirs = 2 * half + 1 - core

        def last(slot, carry):
            tokens = pl.ds(pl.multiple_of(slot * 256, 256), 256)
            product = part[theirs, tokens] + multiply(shared, rows, theirs, slot, 3, 1)
            leaving[at, tokens] = product.astype(BF16)
            return carry

        lax.fori_loop(0, 4, last, 0)
        copy = pltpu.make_async_remote_copy(
            src_ref=leaving.at[at],
            dst_ref=other.at[at],
            send_sem=core_send.at[at],
            recv_sem=core_recv.at[at],
            device_id={"c": 1 - core},
            device_id_type=BY_MESH,
        )
        copy.start()
        copies.append(copy)
    slot_here = ((y * 4 + z) * 4 + x) * 2 + zl
    for at, half in enumerate(halves):
        mine = 2 * half + core

        def last(slot, carry):
            tokens = pl.ds(pl.multiple_of(slot * 256, 256), 256)
            part[mine, tokens] += multiply(shared, rows, mine, slot, 3, 1)
            return carry

        lax.fori_loop(0, 4, last, 0)
        copies[at].wait_recv()
        both = part[mine] + other[at].astype(F32)
        total[at] = pltpu.einshape("abk->bak", both.reshape(16, 64, 256)).astype(BF16)

        def send(step, carry):
            to = tm_peer(place, step)
            pltpu.make_async_remote_copy(
                src_ref=total.at[at, tm_index(to)],
                dst_ref=dst.at[slot_here],
                send_sem=send_sem,
                recv_sem=recv_sem,
                device_id={**to, "zl": half},
                device_id_type=BY_MESH,
            ).start()
            return carry

        lax.fori_loop(at, 64, send, 0, unroll=8 - at)
    own = pltpu.make_async_copy(
        total.at[1, tm_index(tm_peer(place, 0))], dst.at[slot_here], own_sem
    )
    own.start()
    rest = dst.at[pl.ds(0, 127)]
    pltpu.make_async_copy(rest, rest, send_sem).wait()
    pltpu.make_async_copy(rest, rest, recv_sem).wait()
    for copy in copies:
        copy.wait_send()
    own.wait()


SWAP_SEMS = [pltpu.SemaphoreType.DMA] * 3
SHARE_SEMS = [
    pltpu.SemaphoreType.DMA((3, 4)),
    pltpu.SemaphoreType.DMA((3, 4)),
    pltpu.SemaphoreType.DMA,
]
ROWS_SEMS = [
    pltpu.SemaphoreType.DMA((4, 4)),
    pltpu.SemaphoreType.DMA((4, 4)),
    pltpu.SemaphoreType.DMA,
]
CORE_SEMS = [pltpu.SemaphoreType.DMA((2,)), pltpu.SemaphoreType.DMA((2,))]


def whole(*arrays):
    return pl.pallas_call(
        whole_kernel,
        out_shape=jax.ShapeDtypeStruct((128, 16, 256), BF16),
        in_specs=[pl.BlockSpec(memory_space=pltpu.HBM)] * 5,
        out_specs=ANY,
        scratch_shapes=[
            pltpu.VMEM((3, 4, 4, 64, 1024), BF16),
            pltpu.VMEM((3, 16, 64, 1024), BF16),
            pltpu.VMEM((4, 256, 1024), BF16),
            pltpu.VMEM((CHUNKS, 64, 16, WIDTH), BF16),
            pltpu.VMEM((CHUNKS, 64, 16, WIDTH), BF16),
            pltpu.VMEM((16, 64, WIDTH), BF16),
            pltpu.VMEM((3, 4, 64, 1024), BF16),
            pltpu.VMEM((4, 1024, 256), F32),
            pltpu.VMEM((2, 1024, 256), BF16),
            pltpu.VMEM((2, 1024, 256), BF16),
            pltpu.VMEM((2, 64, 16, 256), BF16),
            pltpu.SemaphoreType.DMA((4,)),
            *ROWS_SEMS,
            *CORE_SEMS,
            *SWAP_SEMS,
            *SWAP_SEMS * CHUNKS,
            *SHARE_SEMS * CHUNKS,
        ],
        compiler_params=pltpu.CompilerParams(
            collective_id=1, has_side_effects=True, vmem_limit_bytes=56 << 20
        ),
        name="whole",
    )(*(pltpu.with_memory_space_constraint(array, pltpu.HBM) for array in arrays))


def patch_order():
    z, x, _, slot, c = np.indices((4, 4, 2, 4, 4)).reshape(5, 512)
    return np.eye(256, dtype=np.float32)[4 * (z * 16 + slot * 4 + x) + c]


def per_device(query, key_in, value, grad_out, weights):
    back = whole(query, key_in, value, grad_out, weights).reshape(4, 512, 256)
    place = jnp.asarray(patch_order(), BF16)
    out = jnp.einsum("ytk,tp->ykp", back, place, preferred_element_type=F32)
    return out.reshape(1024, 256).astype(BF16)


def solution(mesh):
    fine = Mesh(mesh.devices.reshape(4, 4, 4, 2, 2), AXES)
    placed = (P(TM, HEAD),) * 4 + (P(None, TM, HEAD),)
    return jax.shard_map(
        per_device, mesh=fine, in_specs=placed, out_specs=P(HEAD, TM), check_vma=False
    )
```

```python
import functools

import jax
import jax.numpy as jnp
import numpy as np
from jax import lax
from jax.experimental import pallas as pl
from jax.experimental.pallas import tpu as pltpu
from jax.sharding import Mesh, PartitionSpec as P

HD = 128
WIDTHS = (512, 256, 256)
STARTS = (0, 512, 768)
CHUNKS = len(WIDTHS)
AXES = ("z", "y", "x", "zl", "c")
TM = AXES[:3]
HEAD = AXES[3:]
BF16 = jnp.bfloat16
F32 = jnp.float32
BY_MESH = pl.DeviceIdType.MESH
ANY = pl.BlockSpec(memory_space=pl.ANY)


def position():
    return lax.axis_index("z"), lax.axis_index("y"), lax.axis_index("x")


def turn(at, by):
    return lax.rem(at + by, jnp.int32(4))


def tm_peer(place, step):
    z, y, x = place
    step = jnp.int32(step)
    by_x, rest = lax.rem(step, jnp.int32(4)), lax.div(step, jnp.int32(4))
    by_y, by_z = lax.rem(rest, jnp.int32(4)), lax.div(rest, jnp.int32(4))
    return {"z": turn(z, by_z), "y": turn(y, by_y), "x": turn(x, by_x)}


def tm_index(at):
    return at["z"] * 16 + at["y"] * 4 + at["x"]


def greet_all(place, zl, core):
    barrier = pltpu.get_barrier_semaphore()

    def greet(half):
        def body(step, carry):
            to = {**tm_peer(place, step), "zl": half}
            pl.semaphore_signal(barrier, inc=1, device_id=to, device_id_type=BY_MESH)
            return carry

        return body

    pl.semaphore_signal(barrier, inc=1, device_id={"c": 1 - core}, device_id_type=BY_MESH)
    lax.fori_loop(1, 64, greet(zl), 0, unroll=7)
    lax.fori_loop(0, 64, greet(1 - zl), 0, unroll=8)
    pl.semaphore_wait(barrier, 128)


def swap_own(place, src, dst, send_sem, recv_sem, own_sem):
    me = tm_index(tm_peer(place, 0))
    own = pltpu.make_async_copy(src.at[me], dst.at[me], own_sem)
    own.start()
    return own


def swap_start(place, src, dst, send_sem, recv_sem, own_sem):
    me = tm_index(tm_peer(place, 0))

    def send(step, carry):
        to = tm_peer(place, step)
        pltpu.make_async_remote_copy(
            src_ref=src.at[tm_index(to)],
            dst_ref=dst.at[me],
            send_sem=send_sem,
            recv_sem=recv_sem,
            device_id=to,
            device_id_type=BY_MESH,
        ).start()
        return carry

    lax.fori_loop(1, 64, send, 0, unroll=7)


def swap_wait(own, src, dst, send_sem, recv_sem):
    most = pl.ds(0, 63)
    pltpu.make_async_copy(src.at[most], src.at[most], send_sem).wait()
    pltpu.make_async_copy(dst.at[most], dst.at[most], recv_sem).wait()
    own.wait()


def share_start(y, src, dst, columns, send_sem, recv_sem, own_sem):
    up, down = (y + 1) % 4, (y + 3) % 4
    own = pltpu.make_async_copy(
        src.at[:, :, :, columns], dst.at[:, y, :, :, columns], own_sem
    )
    own.start()

    def send(block, slot, c, target, lane):
        copy = pltpu.make_async_remote_copy(
            src_ref=block,
            dst_ref=dst.at[:, slot, c, :, columns],
            send_sem=send_sem.at[lane, c],
            recv_sem=recv_sem.at[lane, c],
            device_id={"y": target},
            device_id_type=BY_MESH,
        )
        copy.start()
        return copy

    ups, downs = {}, {}
    for step in range(4):
        c, d = step, (step + 2) % 4
        ups[c] = send(src.at[:, c, :, columns], y, c, up, 0)
        downs[d] = send(src.at[:, d, :, columns], y, d, down, 1)

    far = []

    def forward():
        for step in range(2):
            c, d = step, step + 2
            ups[c].wait_recv()
            far.append(send(dst.at[:, down, c, :, columns], down, c, up, 2))
            downs[d].wait_recv()
            far.append(send(dst.at[:, up, d, :, columns], up, d, down, 2))

    def finish():
        for step in range(2):
            ups[step + 2].wait_recv()
            downs[step].wait_recv()
        for copy in far:
            copy.wait_recv()
        for copy in (*ups.values(), *downs.values(), *far):
            copy.wait_send()
        own.wait()

    return forward, finish


def pack(arrays, into, start, width):
    row = lax.broadcasted_iota(jnp.int32, (64, 64), 0)
    column = lax.broadcasted_iota(jnp.int32, (64, 64), 1)
    wanted = ((row // 4) % 4) * 16 + (row // 16) * 4 + row % 4
    order = jnp.where(column == wanted, 1.0, 0.0).astype(BF16)

    columns = pl.ds(start, width)

    def body(group, carry):
        rows = pl.ds(pl.multiple_of(group * 16, 16), 16)
        block = jnp.concatenate([arrays[at, rows, columns] for at in range(4)], axis=0)
        ordered = jnp.dot(order, block, preferred_element_type=F32).astype(BF16)
        into[pl.ds(group * 4, 4)] = ordered.reshape(4, 16, width)
        return carry

    lax.fori_loop(0, 16, body, 0)


def attend(moved, heads, grads, start, width):
    turned = pltpu.einshape("abk->bak", moved[...].astype(F32))
    heads[:, :, pl.ds(0, width)] = turned.astype(BF16)
    scale = 1.0 / HD**0.5
    row = lax.broadcasted_iota(jnp.int32, (128, 128), 0)
    column = lax.broadcasted_iota(jnp.int32, (128, 128), 1)
    same = row // 64 == column // 64

    def dot(a, b, over_a, over_b):
        return lax.dot_general(
            a, b, (((over_a,), (over_b,)), ((), ())), preferred_element_type=F32
        )

    def body(pair, carry):
        patches = pl.ds(pair * 2, 2)
        for head in range(width // HD):
            lanes = slice(head * HD, (head + 1) * HD)
            q, k, v, g = (
                heads[pl.ds(array * 4 + pair * 2, 2), :, lanes].reshape(128, HD)
                for array in range(4)
            )
            scores = jnp.where(same, dot(q, k, 1, 1) * scale, -1e30)
            weight = jnp.exp(scores - jnp.max(scores, axis=1, keepdims=True))
            probs = weight / jnp.sum(weight, axis=1, keepdims=True)
            probs_b = probs.astype(BF16)
            attended = dot(probs_b, v, 1, 0)
            delta = jnp.sum(g.astype(F32) * attended, axis=1, keepdims=True)
            grad_scores = (probs * (dot(g, v, 1, 1) - delta)).astype(BF16)
            results = (
                dot(grad_scores, k, 1, 0) * scale,
                dot(grad_scores, q, 0, 0) * scale,
                dot(probs_b, g, 0, 0),
            )
            out = pl.ds(start + head * HD, HD)
            for m, result in enumerate(results):
                grads[m, patches, :, out] = result.astype(BF16).reshape(2, 64, HD)
        return carry

    lax.fori_loop(0, 2, body, 0)


def rows_start(place, own_rows, rows, send_sem, recv_sem, own_sem):
    z, y, x = place
    steps = (0, 3, 2, 1)

    def block(b, at_x, part=slice(None)):
        return rows.at[:, ((z + steps[b]) % 4) * 4 + at_x, part]

    def plan(src, dst, axis, target, lane, b):
        return pltpu.make_async_remote_copy(
            src_ref=src,
            dst_ref=dst,
            send_sem=send_sem.at[lane, b],
            recv_sem=recv_sem.at[lane, b],
            device_id={axis: target},
            device_id_type=BY_MESH,
        )

    z_up, z_down, x_up, x_down = (z + 1) % 4, (z + 3) % 4, (x + 1) % 4, (x + 3) % 4
    low, high = pl.ds(0, 32), pl.ds(32, 32)
    z_ups = plan(own_rows, block(0, x), "z", z_up, 0, 0)
    z_downs = plan(own_rows, block(0, x), "z", z_down, 0, 1)
    z_far = (
        plan(block(1, x, low), block(1, x, low), "z", z_up, 0, 2),
        plan(block(3, x, high), block(3, x, high), "z", z_down, 0, 3),
    )
    ups, downs, far = [], [], []
    for b in range(4):
        src = own_rows if b == 0 else block(b, x)
        ups.append(plan(src, block(b, x), "x", x_up, 1, b))
        downs.append(plan(src, block(b, x), "x", x_down, 2, b))
        at, target = (x_down, x_up) if b < 2 else (x_up, x_down)
        far.append(plan(block(b, at), block(b, at), "x", target, 3, b))
    own = pltpu.make_async_copy(own_rows, block(0, x), own_sem)
    own.start()
    ups[0].start()
    downs[0].start()

    def along_z():
        z_ups.start()
        z_downs.start()

    def near():
        for copy, onward, b in ((z_ups, z_far[0], 1), (z_downs, z_far[1], 3)):
            copy.wait_recv()
            onward.start()
            ups[b].start()
            downs[b].start()

    def across():
        for copy in z_far:
            copy.wait_recv()
        ups[2].start()
        downs[2].start()

    def forward(b):
        (ups if b < 2 else downs)[b].wait_recv()
        far[b].start()

    def finish():
        for b in range(4):
            (downs if b < 2 else ups)[b].wait_recv()
            far[b].wait_recv()
        for copy in (z_ups, z_downs, *z_far, *ups, *downs, *far):
            copy.wait_send()
        own.wait()

    return along_z, near, across, forward, finish


def multiply(shared, rows, hg, slot, start, width):
    columns = pl.ds(start, width)
    product = None
    for m in range(3):
        term = lax.dot_general(
            shared[m, slot, :, :, columns].reshape(256, width),
            rows[m, pl.ds(hg * 4, 4), :, columns].reshape(256, width),
            (((1,), (1,)), ((), ())),
            preferred_element_type=F32,
        )
        product = term if product is None else product + term
    return product


def whole_kernel(
    query, key_in, value, grad_out, own_rows, dst, shared, rows, local, heads, grads, part,
    leaving, other, total, *scratch
):
    place = position()
    z, y, x = place
    zl, core = lax.axis_index("zl"), lax.axis_index("c")
    packed, moved, sems = scratch[:CHUNKS], scratch[CHUNKS : 2 * CHUNKS], scratch[2 * CHUNKS :]
    loads = [
        pltpu.make_async_copy(ref, local.at[at], sems[0].at[at])
        for at, ref in enumerate((query, key_in, value, grad_out))
    ]
    for load in loads:
        load.start()
    rows_sems = sems[1:4]
    core_send, core_recv, send_sem, recv_sem, own_sem = sems[4:9]
    swap_sems = [sems[9 + 3 * chunk : 12 + 3 * chunk] for chunk in range(CHUNKS)]
    share_sems = [sems[9 + 3 * chunk : 12 + 3 * chunk] for chunk in range(CHUNKS, 2 * CHUNKS)]
    greet_all(place, zl, core)
    swaps, forwards, finishes = [], [], []

    def swap_out(chunk):
        swap_start(place, packed[chunk], moved[chunk], *swap_sems[chunk])

    def swapped(chunk):
        swap_wait(swaps[chunk], packed[chunk], moved[chunk], *swap_sems[chunk][:2])
        attend(moved[chunk], heads, grads, STARTS[chunk], WIDTHS[chunk])
        columns = pl.ds(STARTS[chunk], WIDTHS[chunk])
        forward, finish = share_start(y, grads, shared, columns, *share_sems[chunk])
        forwards.append(forward)
        finishes.append(finish)

    swaps_first, rows_first = pl.when(zl == 0), pl.when(zl == 1)
    along_z, near, across, pass_on, rows_finish = rows_start(place, own_rows, rows, *rows_sems)
    rows_first(along_z)
    for load in loads:
        load.wait()
    for chunk in range(CHUNKS):
        pack(local, packed[chunk], STARTS[chunk], WIDTHS[chunk])
        swaps.append(swap_own(place, packed[chunk], moved[chunk], *swap_sems[chunk]))
        swaps_first(functools.partial(swap_out, chunk))

    @rows_first
    def _():
        near()
        for chunk in range(CHUNKS):
            swap_out(chunk)

    swapped(0)
    pass_on(0)
    swaps_first(along_z)
    rows_first(across)
    swapped(1)
    forwards[0]()
    swaps_first(near)

    @rows_first
    def _():
        pass_on(1)
        pass_on(3)

    swapped(2)
    forwards[1]()

    @swaps_first
    def _():
        across()
        pass_on(1)
        pass_on(3)

    pass_on(2)
    forwards[2]()
    for finish in finishes[:-1]:
        finish()
    rows_finish()

    def most(at, carry):
        hg, slot = at // 4, at % 4
        part[hg, pl.ds(slot * 256, 256)] = multiply(shared, rows, hg, slot, 0, STARTS[-1])
        return carry

    lax.fori_loop(0, 16, most, 0)
    finishes[-1]()

    halves = (1 - zl, zl)
    copies = []
    for at, half in enumerate(halves):
        theirs = 2 * half + 1 - core

        def last(slot, carry):
            tokens = pl.ds(pl.multiple_of(slot * 256, 256), 256)
            product = part[theirs, tokens] + multiply(shared, rows, theirs, slot, STARTS[-1], WIDTHS[-1])
            leaving[at, tokens] = product.astype(BF16)
            return carry

        lax.fori_loop(0, 4, last, 0)
        copy = pltpu.make_async_remote_copy(
            src_ref=leaving.at[at],
            dst_ref=other.at[at],
            send_sem=core_send.at[at],
            recv_sem=core_recv.at[at],
            device_id={"c": 1 - core},
            device_id_type=BY_MESH,
        )
        copy.start()
        copies.append(copy)
    slot_here = ((y * 4 + z) * 4 + x) * 2 + zl
    for at, half in enumerate(halves):
        mine = 2 * half + core

        def last(slot, carry):
            tokens = pl.ds(pl.multiple_of(slot * 256, 256), 256)
            part[mine, tokens] += multiply(shared, rows, mine, slot, STARTS[-1], WIDTHS[-1])
            return carry

        lax.fori_loop(0, 4, last, 0)
        copies[at].wait_recv()
        both = part[mine] + other[at].astype(F32)
        total[at] = pltpu.einshape("abk->bak", both.reshape(16, 64, 256)).astype(BF16)

        def send(step, carry):
            to = tm_peer(place, step)
            pltpu.make_async_remote_copy(
                src_ref=total.at[at, tm_index(to)],
                dst_ref=dst.at[slot_here],
                send_sem=send_sem,
                recv_sem=recv_sem,
                device_id={**to, "zl": half},
                device_id_type=BY_MESH,
            ).start()
            return carry

        lax.fori_loop(at, 64, send, 0, unroll=8 - at)
    own = pltpu.make_async_copy(
        total.at[1, tm_index(tm_peer(place, 0))], dst.at[slot_here], own_sem
    )
    own.start()
    rest = dst.at[pl.ds(0, 127)]
    pltpu.make_async_copy(rest, rest, send_sem).wait()
    pltpu.make_async_copy(rest, rest, recv_sem).wait()
    for copy in copies:
        copy.wait_send()
    own.wait()


SWAP_SEMS = [pltpu.SemaphoreType.DMA] * 3
SHARE_SEMS = [
    pltpu.SemaphoreType.DMA((3, 4)),
    pltpu.SemaphoreType.DMA((3, 4)),
    pltpu.SemaphoreType.DMA,
]
ROWS_SEMS = [
    pltpu.SemaphoreType.DMA((4, 4)),
    pltpu.SemaphoreType.DMA((4, 4)),
    pltpu.SemaphoreType.DMA,
]
CORE_SEMS = [pltpu.SemaphoreType.DMA((2,)), pltpu.SemaphoreType.DMA((2,))]


def whole(*arrays):
    return pl.pallas_call(
        whole_kernel,
        out_shape=jax.ShapeDtypeStruct((128, 16, 256), BF16),
        in_specs=[pl.BlockSpec(memory_space=pltpu.HBM)] * 5,
        out_specs=ANY,
        scratch_shapes=[
            pltpu.VMEM((3, 4, 4, 64, 1024), BF16),
            pltpu.VMEM((3, 16, 64, 1024), BF16),
            pltpu.VMEM((4, 256, 1024), BF16),
            pltpu.VMEM((16, 64, max(WIDTHS)), BF16),
            pltpu.VMEM((3, 4, 64, 1024), BF16),
            pltpu.VMEM((4, 1024, 256), F32),
            pltpu.VMEM((2, 1024, 256), BF16),
            pltpu.VMEM((2, 1024, 256), BF16),
            pltpu.VMEM((2, 64, 16, 256), BF16),
            *[pltpu.VMEM((64, 16, width), BF16) for width in WIDTHS * 2],
            pltpu.SemaphoreType.DMA((4,)),
            *ROWS_SEMS,
            *CORE_SEMS,
            *SWAP_SEMS,
            *SWAP_SEMS * CHUNKS,
            *SHARE_SEMS * CHUNKS,
        ],
        compiler_params=pltpu.CompilerParams(
            collective_id=1, has_side_effects=True, vmem_limit_bytes=56 << 20
        ),
        name="whole",
    )(*(pltpu.with_memory_space_constraint(array, pltpu.HBM) for array in arrays))


def patch_order():
    z, x, _, slot, c = np.indices((4, 4, 2, 4, 4)).reshape(5, 512)
    return np.eye(256, dtype=np.float32)[4 * (z * 16 + slot * 4 + x) + c]


def per_device(query, key_in, value, grad_out, weights):
    back = whole(query, key_in, value, grad_out, weights).reshape(4, 512, 256)
    place = jnp.asarray(patch_order(), BF16)
    out = jnp.einsum("ytk,tp->ykp", back, place, preferred_element_type=F32)
    return out.reshape(1024, 256).astype(BF16)


def solution(mesh):
    fine = Mesh(mesh.devices.reshape(4, 4, 4, 2, 2), AXES)
    placed = (P(TM, HEAD),) * 4 + (P(None, TM, HEAD),)
    return jax.shard_map(
        per_device, mesh=fine, in_specs=placed, out_specs=P(HEAD, TM), check_vma=False
    )
```
